256 devices in a mesh: row: 4 (over y_lo, core), col: 2 (over y_hi), env: 32 (over x, z).
Axes of the slice: x: 4, y: 4 (y_hi: 2, y_lo: 2; y = y_hi * 2 + y_lo), z: 8, core: 2. Of those that a mesh axis runs over, the one named last changes fastest.
Arguments:
- corner: bfloat16 [4, 2, 1024, 1024], P('row', 'col'), may hold values from -0.1875 to 0.1875
- top_edge: bfloat16 [4, 2, 1024, 32768], P('row', 'col', 'env'), may hold values from -0.03125 to 0.03125
- half_system: bfloat16 [4, 2, 1024, 32768], P('row', 'col', 'env'), may hold values from -0.03125 to 0.03125
- values: float32 [4, 2, 1024], P('row', 'col'), may hold values from 0.5 to 4
- cotangent: bfloat16 [4, 2, 1024, 1024], P('row', 'col'), may hold values from -32 to 32
- parity: int32 [4, 2, 4, 8], P('row', 'col'), may hold values 0 or 1
Outputs:
- grad_corner: bfloat16 [4, 2, 1024, 1024], P('row', 'col', 'env')
- grad_edge: bfloat16 [4, 2, 1024, 32768], P('row', 'col', 'env')
- grad_half: bfloat16 [4, 2, 1024, 32768], P('row', 'col', 'env')
- grad_values: float32 [4, 2, 1024], P('row', 'col', 'env')
The draws below stay inside these ranges and needn't reach their ends.
Inputs may be any that keep to these rules, and one draw needn't show every extreme that they name: `parity`: each entry is the Z2 charge of one block of 128 environment indices.
All inputs are finite; a program needn't handle non-finite values.
Results may differ from the reference program's by a relative error of at most 0.0058.
Values may be sent and summed in bfloat16 or wider, within the bound.
A program may use at most 128 MiB of HBM per device.

```python
import math
import jax
import jax.numpy as jnp
from jax import lax

CHI = 1024
HALF = 32
BLK = 128
NBLK = 8
ROWS = 4
COLS = 2


def touch_ends(drawn, own_key, smallest, high):
    extent = drawn.shape
    index_at = [jax.random.randint(jax.random.fold_in(own_key, axis), (), 0, extent[axis]) for axis in range(len(extent))]
    drawn = drawn.at[tuple(index_at)].set(smallest)
    longest = extent.index(max(extent))
    index_at[longest] = (index_at[longest] + 1) % extent[longest]
    return drawn.at[tuple(index_at)].set(high)


def block_scale(own_key, shape, pieces, smallest, high):
    def one(dim, shards_of):
        heights = jax.random.uniform(jax.random.fold_in(jax.random.fold_in(own_key, 6), dim), (shards_of,), jnp.float32, smallest / len(pieces), high / len(pieces))
        return jnp.repeat(jnp.exp(heights), shape[dim] // shards_of).reshape((-1,) + (1,) * (len(shape) - dim - 1))

    level = one(*pieces[0])
    for cut in pieces[1:]:
        level = level * one(*cut)
    return level


def bell_draw(key, shape, width, limit, shards=(), held_as=jnp.bfloat16):
    level = block_scale(key, shape, shards, -0.22, 0.18) if shards else 1.0
    entries = jax.random.normal(key, shape, jnp.float32) * width * level
    return jnp.minimum(jnp.maximum(entries, -limit), limit).astype(held_as)


def setup_inputs(seed: int = 0) -> dict:
    streams_of = jax.random.split(jax.random.key(seed), 7)
    corner = bell_draw(streams_of[0], (ROWS, COLS, CHI, CHI), CHI ** -0.5, 0.1875, ((0, 4), (1, 2)))
    top_edge = bell_draw(streams_of[1], (ROWS, COLS, CHI, HALF * CHI), (CHI * HALF) ** -0.5, 0.03125, ((0, 4), (1, 2), (2, 32)))
    half_system = bell_draw(streams_of[2], (ROWS, COLS, CHI, CHI * HALF), (CHI * HALF) ** -0.5, 0.03125, ((0, 4), (1, 2), (2, 32)))
    values = jnp.clip(jnp.exp(math.log(4.0) - 2.0794415 * jax.random.uniform(streams_of[3], (ROWS, COLS, CHI), jnp.float32) ** block_scale(streams_of[3], (ROWS, COLS, CHI), ((0, 4), (1, 2)), -0.2, 0.2)), 0.5, 4.0)
    cotangent = bell_draw(streams_of[4], (ROWS, COLS, CHI, CHI), (HALF ** 0.5), 32.0, ((0, 4), (1, 2)))
    parity = touch_ends((jax.random.randint(streams_of[5], (ROWS, COLS, 4, NBLK), 0, 2) < 1).astype(jnp.int32), jax.random.fold_in(streams_of[5], 1), 0, 1)
    return {"corner": corner, "top_edge": top_edge, "half_system": half_system, "values": values, "cotangent": cotangent, "parity": parity}


def charge_masks(parity_site):
    charges = jnp.repeat(parity_site, BLK, axis=1)
    corner_mask = charges[0][:, None] == charges[1][None, :]
    out_mask = charges[2][:, None] == charges[3][None, :]
    return corner_mask, out_mask


def one_site(near_corner, top_edge, half_system, values, cotangent, parity_site):
    corner_mask, out_mask = charge_masks(parity_site)
    masked = jnp.where(corner_mask, near_corner, jnp.zeros_like(near_corner)).astype(jnp.float32)
    lower_half = half_system.reshape(CHI, CHI, HALF).astype(jnp.float32)
    absorbed = jnp.einsum("ab,iak->ibk", masked, lower_half, precision=lax.Precision.HIGHEST).astype(jnp.bfloat16)
    absorbed = lax.optimization_barrier(absorbed)
    flat = absorbed.reshape(CHI, CHI * HALF).astype(jnp.float32)
    edge_mat = top_edge.reshape(CHI * HALF, CHI).astype(jnp.float32)
    weight = values ** -0.5
    grad_new = jnp.where(out_mask, weight[:, None] * cotangent.astype(jnp.float32), jnp.float32(0.0)).astype(jnp.bfloat16)
    grad_new = lax.optimization_barrier(grad_new)
    grad_newf = grad_new.astype(jnp.float32)
    grad_edge = jnp.dot(flat.T, grad_newf, precision=lax.Precision.HIGHEST)
    grad_full = jnp.dot(grad_newf, edge_mat.T, precision=lax.Precision.HIGHEST)
    pair_sums = jnp.sum(flat * grad_full, axis=1)
    grad_values = -0.5 * pair_sums / values
    grad_back = lax.optimization_barrier(grad_full.astype(jnp.bfloat16))
    grad_back = grad_back.astype(jnp.float32).reshape(CHI, CHI, HALF)
    grad_half = jnp.einsum("ab,ibk->iak", masked, grad_back, precision=lax.Precision.HIGHEST)
    grad_half = grad_half.astype(jnp.bfloat16).reshape(CHI, CHI * HALF)
    summed = jnp.einsum("iak,ibk->ab", lower_half, grad_back, precision=lax.Precision.HIGHEST)
    grad_corner = jnp.where(corner_mask, summed, jnp.float32(0.0)).astype(jnp.bfloat16)
    grad_edge = grad_edge.astype(jnp.bfloat16).reshape(CHI, HALF * CHI)
    return grad_corner, grad_edge, grad_half, grad_values


def reference(corner, top_edge, half_system, values, cotangent, parity):
    corner_grid = [[None] * COLS for row_index in range(ROWS)]
    edge_grid = [[None] * COLS for row_index in range(ROWS)]
    half_grid = [[None] * COLS for row_index in range(ROWS)]
    value_grid = [[None] * COLS for row_index in range(ROWS)]
    for row_index in range(ROWS):
        for col_index in range(COLS):
            left_col = (col_index - 1) % COLS
            below_row = (row_index + 1) % ROWS
            results = one_site(corner[row_index, left_col], top_edge[row_index, col_index],
                               half_system[below_row, col_index], values[row_index, col_index],
                               cotangent[row_index, col_index], parity[row_index, col_index])
            corner_grid[row_index][left_col] = results[0]
            edge_grid[row_index][col_index] = results[1]
            half_grid[below_row][col_index] = results[2]
            value_grid[row_index][col_index] = results[3]

    def stacked(grid):
        return jnp.stack([jnp.stack(row_list) for row_list in grid])

    return stacked(corner_grid), stacked(edge_grid), stacked(half_grid), stacked(value_grid)
```

```python
import functools

import jax
import jax.numpy as jnp
from jax import lax
from jax.experimental import pallas as pl
from jax.experimental.pallas import tpu as pltpu
from jax.sharding import PartitionSpec as P

CHI = 1024
HALF = 32
BLK = 128
NBLK = CHI // BLK
LANE = 128
SUB = 4
GRP = CHI // SUB
NX, NZ = 4, 8
ROWS_A = 32
QN = 4
QW = CHI // QN
KQ = HALF // QN
MESH = pl.DeviceIdType.MESH
F32 = jnp.float32
BF16 = jnp.bfloat16


def tile_mix(tiles):
    lane = lax.broadcasted_iota(jnp.int32, tiles[0].shape, 1)
    low = lane < 64
    even = (lane // 32) % 2 == 0
    roll = lambda t, by: pltpu.roll(t, by, 1)
    x0, x1, x2, x3 = tiles
    y0 = jnp.where(low, x0, roll(x2, 64))
    y2 = jnp.where(low, roll(x0, 64), x2)
    y1 = jnp.where(low, x1, roll(x3, 64))
    y3 = jnp.where(low, roll(x1, 64), x3)
    z0 = jnp.where(even, y0, roll(y1, 32))
    z1 = jnp.where(even, roll(y0, 96), y1)
    z2 = jnp.where(even, y2, roll(y3, 32))
    z3 = jnp.where(even, roll(y2, 96), y3)
    return z0, z1, z2, z3


def dot_nn(a, b):
    return lax.dot_general(a, b, (((1,), (0,)), ((), ())), preferred_element_type=F32)


def dot_nt(a, b):
    return lax.dot_general(a, b, (((1,), (1,)), ((), ())), preferred_element_type=F32)


def dot_tn(a, b):
    return lax.dot_general(a, b, (((0,), (0,)), ((), ())), preferred_element_type=F32)


def at(start, size):
    return pl.ds(pl.multiple_of(start, size), size)


def loop(n, body):
    lax.fori_loop(0, n, lambda i, c: (body(i), c)[1], 0)


def kernel(
    nr, nc, ne,
    corner, te, lh, gn_in, ch, vals,
    gc_out, ge_out, gh_out, gv_out,
    TE, GN, LHB, CR, CHR, GFS, R, AS, G, NCP, LHM, GFM, S, LM, F, GCB, P1, P1S, P2, PSA, PSS, PSR,
    te_sem, in_sem, out_sem, cn_send, cn_recv, ch_send, ch_recv,
    gf_send, gf_recv, ab_send, ab_recv, p1_send, p1_recv, p2_send, p2_recv, ps_send, ps_recv,
):
    r, c, e = lax.axis_index("row"), lax.axis_index("col"), lax.axis_index("env")
    rp, rm = lax.rem(r + 1, nr), lax.rem(r + nr - 1, nr)
    cp, cm = lax.rem(c + 1, nc), lax.rem(c + nc - 1, nc)
    x, z = e // NZ, lax.rem(e, NZ)

    def dev(row, col, env):
        return {"row": row, "col": col, "env": env}

    def remote(src, dst, send, recv, where):
        return pltpu.make_async_remote_copy(
            src_ref=src, dst_ref=dst, send_sem=send, recv_sem=recv, device_id=where, device_id_type=MESH
        )

    barrier = pltpu.get_barrier_semaphore()

    def greet(where):
        pl.semaphore_signal(barrier, inc=1, device_id=where, device_id_type=MESH)

    def greet_env(s):
        greet(dev(rp, c, s))
        greet(dev(rm, c, s))

    def greet_z(s):
        greet(dev(rp, cp, x * NZ + s))
        greet(dev(rm, cm, x * NZ + s))

    def greet_x(s):
        greet(dev(r, c, lax.rem(x + 1 + s, NX) * NZ + z))

    loop(ne, greet_env)
    loop(NZ, greet_z)
    loop(NX - 1, greet_x)

    gn_copy = pltpu.make_async_copy(gn_in, GN, in_sem.at[0])
    gn_copy.start()

    def load_edge(k):
        pltpu.make_async_copy(
            te.at[:, at(k * CHI, CHI)], TE.at[at(k * ROWS_A, ROWS_A), :], te_sem.at[k // KQ]
        ).start()

    loop(HALF, load_edge)
    lh_copy = pltpu.make_async_copy(lh, LHB, in_sem.at[1])
    lh_copy.start()
    gn_copy.wait()

    pl.semaphore_wait(barrier, 2 * ne + 2 * NZ + NX - 1)

    remote(ch, CHR, ch_send, ch_recv, dev(rp, c, e)).start()

    def send_corner(g):
        rows = at(g * BLK, BLK)
        remote(corner.at[rows, :], CR.at[rows, :], cn_send, cn_recv.at[g], dev(rp, cp, e)).start()

    def edge_chunk(q):
        cols = at(q * QW, QW)
        whole = TE.at[cols, :]
        pltpu.make_async_copy(whole, whole, te_sem.at[q]).wait()

        def rows_of(m):
            rows = at(m * 256, 256)
            GFS[rows, cols] = dot_nt(GN[rows, :], TE[cols, :]).astype(BF16)

        loop(CHI // 256, rows_of)

        def send(j):
            s = lax.rem(e + j, ne)
            remote(
                GFS.at[at(s * ROWS_A, ROWS_A), cols], R.at[at(e * ROWS_A, ROWS_A), cols],
                gf_send.at[q], gf_recv.at[q], dev(rp, c, s),
            ).start()

        loop(ne, send)

    loop(NBLK, send_corner)
    loop(QN, edge_chunk)

    lh_copy.wait()

    def spread(g):
        for u in range(8):
            S[at((g * 8 + u) * ROWS_A, ROWS_A), :] = LHB[:, at((g * 8 + u) * LANE, LANE)].astype(F32)

    loop(GRP // 8, spread)

    def turn(i):
        t = S[pl.ds(i, GRP, stride=ROWS_A), :].T
        for s in range(SUB):
            for h in range(GRP // LANE):
                LM[s * (GRP // LANE) + h, pl.ds(i, HALF, stride=ROWS_A), :] = t[
                    s * HALF:(s + 1) * HALF, h * LANE:(h + 1) * LANE]

    loop(ROWS_A, turn)

    def narrow(k):
        rows = at(k * ROWS_A, ROWS_A)
        for t in range(CHI // LANE):
            LHM[rows, t * LANE:(t + 1) * LANE] = LM[t, rows, :].astype(BF16)

    loop(HALF, narrow)

    remote(CHR, CHR, ch_send, ch_recv, dev(rp, c, e)).wait_recv()

    def corner_rows(g):
        rows = at(g * BLK, BLK)
        part = CR.at[rows, :]
        remote(part, part, cn_send, cn_recv.at[g], dev(rp, cp, e)).wait_recv()
        charge = CHR[0:1, rows]
        for t in range(CHI // LANE):
            lanes = slice(t * LANE, (t + 1) * LANE)
            same = charge == CHR[1:2, lanes]
            F[t, rows, :] = jnp.where(same, CR[rows, lanes].astype(F32), 0.0)
            for s in range(SUB):
                NCP[at(s * GRP + g * (BLK // SUB), BLK // SUB), lanes] = F[
                    t, pl.ds(g * BLK + s, BLK // SUB, stride=SUB), :].astype(BF16)

    loop(NBLK, corner_rows)

    def absorb_chunk(q):
        cols = at(q * QW, QW)

        def columns_of(n):
            t = dot_nn(LHM[cols, :], NCP[:, at(n * 256, 256)])
            for k2 in range(KQ // 4):
                for d2 in range(2):
                    mixed = tile_mix([
                        t[(k2 * 4 + k4) * ROWS_A:(k2 * 4 + k4 + 1) * ROWS_A, d2 * LANE:(d2 + 1) * LANE]
                        for k4 in range(4)])
                    for d4 in range(4):
                        AS[at(((n * 2 + d2) * 4 + d4) * ROWS_A, ROWS_A), at(q * QW + k2 * LANE, LANE)] = (
                            mixed[d4].astype(BF16))

        loop(CHI // 256, columns_of)

        def send(j):
            s = lax.rem(e + j, ne)
            remote(
                AS.at[at(s * ROWS_A, ROWS_A), cols], G.at[at(e * ROWS_A, ROWS_A), cols],
                ab_send.at[q], ab_recv.at[q], dev(rm, c, s),
            ).start()

        loop(ne, send)

    loop(QN, absorb_chunk)

    PSA[...] = jnp.zeros_like(PSA)

    def half_chunk(q):
        cols = at(q * QW, QW)
        whole = R.at[:, cols]
        remote(whole, whole, gf_send.at[q], gf_recv.at[q], dev(rp, c, e)).wait_recv()

        def regroup(d):
            for k2 in range(KQ // 4):
                lanes = at(q * QW + k2 * LANE, LANE)
                tiles = []
                total = PSA[...]
                for d4 in range(4):
                    rows = at((d * 4 + d4) * ROWS_A, ROWS_A)
                    tile = R[rows, lanes].astype(F32)
                    total = total + tile * AS[rows, lanes].astype(F32)
                    tiles.append(tile)
                PSA[...] = total
                mixed = tile_mix(tiles)
                for k4 in range(4):
                    GFM[at((q * KQ + k2 * 4 + k4) * ROWS_A, ROWS_A), at(d * LANE, LANE)] = mixed[k4].astype(BF16)

        loop(CHI // LANE, regroup)

        def half_cols(n):
            t = dot_nt(GFM[cols, :], NCP[at(n * 256, 256), :])
            for h in range(2):
                LM[n * 2 + h, cols, :] = t[:, h * LANE:(h + 1) * LANE]

        loop(CHI // 256, half_cols)

    loop(QN, half_chunk)

    PSS[...] = jnp.broadcast_to(jnp.sum(PSA[...], axis=1, keepdims=True), (ROWS_A, LANE))
    ps_copy = remote(PSS, PSR, ps_send, ps_recv, dev(rm, c, e))
    ps_copy.start()

    def corner_part(s):
        t = dot_tn(LHM[:, at(s * GRP, GRP)], GFM[...])
        for g in range(NBLK):
            for h in range(CHI // LANE):
                same = CHR[0:1, g * BLK:(g + 1) * BLK] == CHR[1:2, h * LANE:(h + 1) * LANE]
                part = t[g * (BLK // SUB):(g + 1) * (BLK // SUB), h * LANE:(h + 1) * LANE]
                F[h, pl.ds(g * BLK + s, BLK // SUB, stride=SUB), :] = jnp.where(same, part, 0.0)

    loop(SUB, corner_part)

    def corner_narrow(g):
        rows = at(g * 32, 32)
        for t in range(CHI // LANE):
            GCB[rows, t * LANE:(t + 1) * LANE] = F[t, rows, :].astype(BF16)

    loop(CHI // 32, corner_narrow)
    span = CHI // NX

    def send_x(j):
        to = lax.rem(x + 1 + j, NX)
        remote(
            GCB.at[at(to * span, span), :], P1.at[j], p1_send, p1_recv, dev(r, c, to * NZ + z)
        ).start()

    loop(NX - 1, send_x)

    def turn_back(i):
        t = jnp.concatenate([
            jnp.concatenate([
                LM[s * (GRP // LANE) + h, pl.ds(i, HALF, stride=ROWS_A), :] for h in range(GRP // LANE)
            ], axis=1) for s in range(SUB)], axis=0)
        S[pl.ds(i, GRP, stride=ROWS_A), :] = t.T

    loop(ROWS_A, turn_back)

    def gather(g):
        for u in range(8):
            LHB[:, at((g * 8 + u) * LANE, LANE)] = S[at((g * 8 + u) * ROWS_A, ROWS_A), :].astype(BF16)

    loop(GRP // 8, gather)
    gh_copy = pltpu.make_async_copy(LHB, gh_out, in_sem.at[1])
    gh_copy.start()

    remote(P1, P1, p1_send, p1_recv, dev(r, c, e)).wait_recv()

    def sum_x(g):
        rows = at(g * 32, 32)
        for t in range(CHI // LANE):
            lanes = slice(t * LANE, (t + 1) * LANE)
            total = F[t, at(x * span + g * 32, 32), :]
            for j in range(NX - 1):
                total = total + P1[j, rows, lanes].astype(F32)
            P1S[rows, lanes] = total.astype(BF16)

    loop(span // 32, sum_x)

    def send_z(j):
        to = lax.rem(z + j, NZ)
        remote(
            P1S.at[at(to * ROWS_A, ROWS_A), :], P2.at[at(z * ROWS_A, ROWS_A), :],
            p2_send, p2_recv, dev(rm, cm, x * NZ + to),
        ).start()

    loop(NZ, send_z)

    def edge_grad(q):
        cols = at(q * QW, QW)
        whole = G.at[:, cols]
        remote(whole, whole, ab_send.at[q], ab_recv.at[q], dev(rm, c, e)).wait_recv()
        TE[cols, :] = dot_tn(G[:, cols], GN[...]).astype(BF16)

        def store(j):
            k = q * KQ + j
            pltpu.make_async_copy(
                TE.at[at(k * ROWS_A, ROWS_A), :], ge_out.at[:, at(k * CHI, CHI)], out_sem
            ).start()

        loop(KQ, store)

    loop(QN, edge_grad)

    remote(P2, P2, p2_send, p2_recv, dev(rm, cm, e)).wait_recv()
    for t in range(CHI // LANE):
        lanes = slice(t * LANE, (t + 1) * LANE)
        total = P2[0:ROWS_A, lanes].astype(F32)
        for j in range(1, NZ):
            total = total + P2[j * ROWS_A:(j + 1) * ROWS_A, lanes].astype(F32)
        gc_out[:, lanes] = total.astype(BF16)

    ps_copy.wait_recv()
    own = lax.broadcasted_iota(jnp.int32, (ROWS_A, LANE), 0) == lax.broadcasted_iota(jnp.int32, (ROWS_A, LANE), 1)
    sums = jnp.sum(jnp.where(own, PSR[...], 0.0), axis=0, keepdims=True)
    gv_out[...] = -0.5 * sums[:, :ROWS_A] / vals[...]

    ps_copy.wait_send()
    remote(ch, CHR, ch_send, ch_recv, dev(rp, c, e)).wait_send()
    remote(CR, CR, cn_send, cn_recv.at[0], dev(rp, cp, e)).wait_send()
    for q in range(QN):
        part = GFS.at[:, q * QW:(q + 1) * QW]
        remote(part, part, gf_send.at[q], gf_recv.at[q], dev(rp, c, e)).wait_send()
        part = AS.at[:, q * QW:(q + 1) * QW]
        remote(part, part, ab_send.at[q], ab_recv.at[q], dev(rm, c, e)).wait_send()
    remote(P1, P1, p1_send, p1_recv, dev(r, c, e)).wait_send()
    remote(P1S, P1S, p2_send, p2_recv, dev(rm, cm, e)).wait_send()
    gh_copy.wait()
    pltpu.make_async_copy(TE, TE, out_sem).wait()


def absorb_backward(sizes, corner, te, lh, gn, ch, vals):
    nr, nc, ne = sizes
    hbm = pl.BlockSpec(memory_space=pl.ANY)
    vmem = pl.BlockSpec(memory_space=pltpu.VMEM)
    dma = pltpu.SemaphoreType.DMA
    square = pltpu.VMEM((CHI, CHI), BF16)
    tiles = pltpu.VMEM((CHI // LANE, CHI, LANE), F32)
    scratch = [
        square, square, pltpu.VMEM((ROWS_A, CHI * HALF), BF16), square, pltpu.VMEM((8, CHI), jnp.int32),
        square, square, square, square, square, square, square,
        pltpu.VMEM((GRP * ROWS_A, LANE), F32), tiles, tiles, square,
        pltpu.VMEM((NX - 1, CHI // NX, CHI), BF16), pltpu.VMEM((CHI // NX, CHI), BF16),
        pltpu.VMEM((NZ * ROWS_A, CHI), BF16),
        pltpu.VMEM((ROWS_A, LANE), F32), pltpu.VMEM((ROWS_A, LANE), F32), pltpu.VMEM((ROWS_A, LANE), F32),
        dma((QN,)), dma((2,)), dma, dma, dma((NBLK,)), dma, dma,
        dma((QN,)), dma((QN,)), dma((QN,)), dma((QN,)), dma, dma, dma, dma, dma, dma,
    ]
    return pl.pallas_call(
        functools.partial(kernel, nr, nc, ne),
        out_shape=(
            jax.ShapeDtypeStruct((ROWS_A, CHI), BF16),
            jax.ShapeDtypeStruct((ROWS_A, HALF * CHI), BF16),
            jax.ShapeDtypeStruct((ROWS_A, CHI * HALF), BF16),
            jax.ShapeDtypeStruct((1, ROWS_A), F32),
        ),
        in_specs=[hbm, hbm, hbm, hbm, hbm, vmem],
        out_specs=(vmem, hbm, hbm, vmem),
        scratch_shapes=scratch,
        compiler_params=pltpu.CompilerParams(
            collective_id=0, has_side_effects=True, vmem_limit_bytes=60 * 1024 * 1024
        ),
    )(corner, te, lh, gn, ch, vals)


def shards(sizes, corner, top_edge, half_system, values, cotangent, parity):
    rows = top_edge.shape[2]
    charges = jnp.repeat(parity[0, 0], BLK, axis=1)
    out_mask = charges[2][:, None] == charges[3][None, :]
    weight = values[0, 0] ** (-0.5)
    grad_new = jnp.where(out_mask, weight[:, None] * cotangent[0, 0].astype(F32), 0.0).astype(BF16)
    ch = jnp.concatenate([charges, charges], axis=0)
    own = lax.dynamic_slice_in_dim(values[0, 0], lax.axis_index("env") * rows, rows, 0)[None, :]
    gc, ge, gh, gv = absorb_backward(
        sizes, corner[0, 0], top_edge[0, 0], half_system[0, 0], grad_new, ch, own
    )
    return gc[None, None], ge[None, None], gh[None, None], gv[None]


def solution(mesh):
    placed = (
        P("row", "col", None, None),
        P("row", "col", "env", None),
        P("row", "col", "env", None),
        P("row", "col", None),
        P("row", "col", None, None),
        P("row", "col", None, None),
    )
    sizes = (mesh.shape["row"], mesh.shape["col"], mesh.shape["env"])
    return jax.shard_map(
        functools.partial(shards, sizes),
        mesh=mesh,
        in_specs=placed,
        out_specs=(
            P("row", "col", "env", None),
            P("row", "col", "env", None),
            P("row", "col", "env", None),
            P("row", "col", "env"),
        ),
        check_vma=False,
    )
```

```python
import functools

import jax
import jax.numpy as jnp
from jax import lax
from jax.experimental import pallas as pl
from jax.experimental.pallas import tpu as pltpu
from jax.sharding import PartitionSpec as P

CHI = 1024
HALF = 32
BLK = 128
NBLK = CHI // BLK
LANE = 128
SUB = 4
GRP = CHI // SUB
NX, NZ = 4, 8
ROWS_A = 32
QN = 4
QW = CHI // QN
KQ = HALF // QN
MESH = pl.DeviceIdType.MESH
F32 = jnp.float32
BF16 = jnp.bfloat16


def tile_mix(tiles):
    lane = lax.broadcasted_iota(jnp.int32, tiles[0].shape, 1)
    low = lane < 64
    even = (lane // 32) % 2 == 0
    roll = lambda t, by: pltpu.roll(t, by, 1)
    x0, x1, x2, x3 = tiles
    y0 = jnp.where(low, x0, roll(x2, 64))
    y2 = jnp.where(low, roll(x0, 64), x2)
    y1 = jnp.where(low, x1, roll(x3, 64))
    y3 = jnp.where(low, roll(x1, 64), x3)
    z0 = jnp.where(even, y0, roll(y1, 32))
    z1 = jnp.where(even, roll(y0, 96), y1)
    z2 = jnp.where(even, y2, roll(y3, 32))
    z3 = jnp.where(even, roll(y2, 96), y3)
    return z0, z1, z2, z3


def dot_nn(a, b):
    return lax.dot_general(a, b, (((1,), (0,)), ((), ())), preferred_element_type=F32)


def dot_nt(a, b):
    return lax.dot_general(a, b, (((1,), (1,)), ((), ())), preferred_element_type=F32)


def dot_tn(a, b):
    return lax.dot_general(a, b, (((0,), (0,)), ((), ())), preferred_element_type=F32)


def at(start, size):
    return pl.ds(pl.multiple_of(start, size), size)


def loop(n, body):
    lax.fori_loop(0, n, lambda i, c: (body(i), c)[1], 0)


def kernel(
    nr, nc, ne,
    corner, te, lh, cot, vals, par,
    gc_out, ge_out, gh_out, gv_out,
    TE, GN, LHB, CR, CH, CHR, ACC, GFS, R, AS, G, NCP, LHM, GFM, S, LM, F, GCB, P1, P1S, P2, PSA, PSS, PSR,
    te_sem, ct_sem, in_sem, out_sem, cn_send, cn_recv, ch_send, ch_recv,
    gf_send, gf_recv, ab_send, ab_recv, p1_send, p1_recv, p2_send, p2_recv, ps_send, ps_recv,
):
    r, c, e = lax.axis_index("row"), lax.axis_index("col"), lax.axis_index("env")
    rp, rm = lax.rem(r + 1, nr), lax.rem(r + nr - 1, nr)
    cp, cm = lax.rem(c + 1, nc), lax.rem(c + nc - 1, nc)
    x, z = e // NZ, lax.rem(e, NZ)

    def dev(row, col, env):
        return {"row": row, "col": col, "env": env}

    def remote(src, dst, send, recv, where):
        return pltpu.make_async_remote_copy(
            src_ref=src, dst_ref=dst, send_sem=send, recv_sem=recv, device_id=where, device_id_type=MESH
        )

    barrier = pltpu.get_barrier_semaphore()

    def greet(where):
        pl.semaphore_signal(barrier, inc=1, device_id=where, device_id_type=MESH)

    def greet_env(s):
        greet(dev(rm, c, s))

    def greet_z(s):
        greet(dev(rp, cp, x * NZ + s))

    def greet_x(s):
        greet(dev(r, c, lax.rem(x + 1 + s, NX) * NZ + z))

    def turned(m):
        return lax.rem(e // (ne // QN) + m, QN)

    def load_cot(m):
        rows = at(turned(m) * QW, QW)
        pltpu.make_async_copy(cot.at[rows, :], GN.at[rows, :], ct_sem.at[turned(m)]).start()

    def load_edge(k):
        pltpu.make_async_copy(
            te.at[:, at(k * CHI, CHI)], TE.at[at(k * ROWS_A, ROWS_A), :], te_sem.at[k // KQ]
        ).start()

    loop(1, load_cot)
    loop(KQ, load_edge)
    loop(ne, greet_env)
    loop(NZ, greet_z)
    loop(NX - 1, greet_x)
    greet(dev(rm, cm, e))
    loop(QN - 1, lambda m: load_cot(m + 1))
    loop(HALF - KQ, lambda k: load_edge(k + KQ))
    lh_copy = pltpu.make_async_copy(lh, LHB, in_sem)
    lh_copy.start()

    for role in range(4):
        for g in range(NBLK):
            CH[role:role + 1, g * BLK:(g + 1) * BLK] = jnp.broadcast_to(par[role:role + 1, g:g + 1], (1, BLK))

    def weigh(m):
        rows = at(turned(m) * QW, QW)
        part = GN.at[rows, :]
        pltpu.make_async_copy(part, part, ct_sem.at[turned(m)]).wait()

        def block(g):
            rows = at(turned(m) * QW + g * BLK, BLK)
            weight = jnp.broadcast_to(lax.rsqrt(vals[0:1, rows]), (BLK, BLK)).T
            charge = CH[2:3, rows]
            for t in range(NBLK):
                lanes = slice(t * BLK, (t + 1) * BLK)
                keep = charge == CH[3:4, lanes]
                GN[rows, lanes] = jnp.where(keep, weight * GN[rows, lanes].astype(F32), 0.0).astype(BF16)

        loop(QW // BLK, block)

    def send_corner(g):
        rows = at(g * BLK, BLK)
        remote(corner.at[rows, :], CR.at[rows, :], cn_send, cn_recv.at[g], dev(rp, cp, e)).start()

    def edge_rows(q, m):
        rows = at(turned(m) * QW, QW)
        cols = at(q * QW, QW)
        GFS[rows, cols] = dot_nt(GN[rows, :], TE[cols, :]).astype(BF16)

    def send_full(q, m):
        def send(j):
            s = turned(m) * (ne // QN) + lax.rem(e + j, ne // QN)
            remote(
                GFS.at[at(s * ROWS_A, ROWS_A), at(q * QW, QW)], R.at[at(e * ROWS_A, ROWS_A), at(q * QW, QW)],
                gf_send.at[q], gf_recv.at[q], dev(rp, c, s),
            ).start()

        loop(ne // QN, send)

    def edge_ready(q):
        whole = TE.at[at(q * QW, QW), :]
        pltpu.make_async_copy(whole, whole, te_sem.at[q]).wait()

    weigh(0)
    edge_ready(0)
    edge_rows(0, 0)
    pl.semaphore_wait(barrier, ne + NZ + NX)
    send_full(0, 0)
    remote(CH, CHR, ch_send, ch_recv, dev(rp, c, e)).start()
    loop(NBLK, send_corner)

    def edge_first(m):
        weigh(m + 1)
        edge_rows(0, m + 1)
        send_full(0, m + 1)

    loop(QN - 1, edge_first)

    def edge_chunk(q):
        edge_ready(q + 1)

        def part(m):
            edge_rows(q + 1, m)
            send_full(q + 1, m)

        loop(QN, part)

    loop(QN - 1, edge_chunk)

    lh_copy.wait()

    def spread(g):
        for u in range(8):
            S[at((g * 8 + u) * ROWS_A, ROWS_A), :] = LHB[:, at((g * 8 + u) * LANE, LANE)].astype(F32)

    loop(GRP // 8, spread)

    def turn(i):
        t = S[pl.ds(i, GRP, stride=ROWS_A), :].T
        for s in range(SUB):
            for h in range(GRP // LANE):
                LM[s * (GRP // LANE) + h, pl.ds(i, HALF, stride=ROWS_A), :] = t[
                    s * HALF:(s + 1) * HALF, h * LANE:(h + 1) * LANE]

    loop(ROWS_A, turn)

    def narrow(k):
        rows = at(k * ROWS_A, ROWS_A)
        for t in range(CHI // LANE):
            LHM[rows, t * LANE:(t + 1) * LANE] = LM[t, rows, :].astype(BF16)

    loop(HALF, narrow)

    def half_chunk(q):
        cols = at(q * QW, QW)
        whole = R.at[:, cols]
        remote(whole, whole, gf_send.at[q], gf_recv.at[q], dev(rp, c, e)).wait_recv()

        def regroup(d):
            for k2 in range(KQ // 4):
                lanes = at(q * QW + k2 * LANE, LANE)
                mixed = tile_mix([
                    R[at((d * 4 + d4) * ROWS_A, ROWS_A), lanes].astype(F32) for d4 in range(4)])
                for k4 in range(4):
                    GFM[at((q * KQ + k2 * 4 + k4) * ROWS_A, ROWS_A), at(d * LANE, LANE)] = mixed[k4].astype(BF16)

        loop(CHI // LANE, regroup)

        def add(s):
            rows = at(s * GRP, GRP)
            ACC[rows, :] = ACC[rows, :] + dot_tn(LHM[cols, rows], GFM[cols, :])

        loop(SUB, add)

    def clear(g):
        rows = at(g * 32, 32)
        ACC[rows, :] = jnp.zeros((32, CHI), F32)

    loop(CHI // 32, clear)
    loop(QN - 1, half_chunk)

    remote(CHR, CHR, ch_send, ch_recv, dev(rp, c, e)).wait_recv()

    def corner_rows(g):
        rows = at(g * BLK, BLK)
        part = CR.at[rows, :]
        remote(part, part, cn_send, cn_recv.at[g], dev(rp, cp, e)).wait_recv()
        charge = CHR[0:1, rows]
        for t in range(CHI // LANE):
            lanes = slice(t * LANE, (t + 1) * LANE)
            same = charge == CHR[1:2, lanes]
            F[t, rows, :] = jnp.where(same, CR[rows, lanes].astype(F32), 0.0)
            for s in range(SUB):
                NCP[at(s * GRP + g * (BLK // SUB), BLK // SUB), lanes] = F[
                    t, pl.ds(g * BLK + s, BLK // SUB, stride=SUB), :].astype(BF16)

    loop(NBLK, corner_rows)

    def absorb_chunk(q):
        cols = at(q * QW, QW)

        def columns_of(n):
            t = dot_nn(LHM[cols, :], NCP[:, at(n * 256, 256)])
            for k2 in range(KQ // 4):
                for d2 in range(2):
                    mixed = tile_mix([
                        t[(k2 * 4 + k4) * ROWS_A:(k2 * 4 + k4 + 1) * ROWS_A, d2 * LANE:(d2 + 1) * LANE]
                        for k4 in range(4)])
                    for d4 in range(4):
                        AS[at(((n * 2 + d2) * 4 + d4) * ROWS_A, ROWS_A), at(q * QW + k2 * LANE, LANE)] = (
                            mixed[d4].astype(BF16))

        loop(CHI // 256, columns_of)

        def send(j):
            s = lax.rem(e + j, ne)
            remote(
                AS.at[at(s * ROWS_A, ROWS_A), cols], G.at[at(e * ROWS_A, ROWS_A), cols],
                ab_send.at[q], ab_recv.at[q], dev(rm, c, s),
            ).start()

        loop(ne, send)

    loop(QN, absorb_chunk)

    half_chunk(QN - 1)

    def corner_part(s):
        def block(g):
            for h in range(CHI // LANE):
                lanes = slice(h * LANE, (h + 1) * LANE)
                same = CHR[0:1, at(g * BLK, BLK)] == CHR[1:2, lanes]
                part = ACC[at(s * GRP + g * (BLK // SUB), BLK // SUB), lanes]
                F[h, pl.ds(g * BLK + s, BLK // SUB, stride=SUB), :] = jnp.where(same, part, 0.0)

        loop(NBLK, block)

    loop(SUB, corner_part)

    def corner_narrow(g):
        rows = at(g * 32, 32)
        for t in range(CHI // LANE):
            GCB[rows, t * LANE:(t + 1) * LANE] = F[t, rows, :].astype(BF16)

    loop(CHI // 32, corner_narrow)
    span = CHI // NX

    def send_x(j):
        to = lax.rem(x + 1 + j, NX)
        remote(
            GCB.at[at(to * span, span), :], P1.at[j], p1_send, p1_recv, dev(r, c, to * NZ + z)
        ).start()

    loop(NX - 1, send_x)

    def pair(d):
        rows = at(d * ROWS_A, ROWS_A)
        total = PSA[...]
        for t in range(CHI // LANE):
            lanes = slice(t * LANE, (t + 1) * LANE)
            total = total + R[rows, lanes].astype(F32) * AS[rows, lanes].astype(F32)
        PSA[...] = total

    PSA[...] = jnp.zeros_like(PSA)
    loop(ne, pair)
    PSS[...] = jnp.broadcast_to(jnp.sum(PSA[...], axis=1, keepdims=True), (ROWS_A, LANE))
    ps_copy = remote(PSS, PSR, ps_send, ps_recv, dev(rm, c, e))
    ps_copy.start()

    def half_rows(q):
        cols = at(q * QW, QW)

        def half_cols(n):
            t = dot_nt(GFM[cols, :], NCP[at(n * 256, 256), :])
            for h in range(2):
                LM[n * 2 + h, cols, :] = t[:, h * LANE:(h + 1) * LANE]

        loop(CHI // 256, half_cols)

    loop(QN, half_rows)

    def turn_back(i):
        t = jnp.concatenate([
            jnp.concatenate([
                LM[s * (GRP // LANE) + h, pl.ds(i, HALF, stride=ROWS_A), :] for h in range(GRP // LANE)
            ], axis=1) for s in range(SUB)], axis=0)
        S[pl.ds(i, GRP, stride=ROWS_A), :] = t.T

    loop(ROWS_A, turn_back)

    def gather(g):
        for u in range(8):
            LHB[:, at((g * 8 + u) * LANE, LANE)] = S[at((g * 8 + u) * ROWS_A, ROWS_A), :].astype(BF16)

    loop(GRP // 8, gather)
    gh_copy = pltpu.make_async_copy(LHB, gh_out, in_sem)
    gh_copy.start()

    remote(P1, P1, p1_send, p1_recv, dev(r, c, e)).wait_recv()

    def sum_x(g):
        rows = at(g * 32, 32)
        for t in range(CHI // LANE):
            lanes = slice(t * LANE, (t + 1) * LANE)
            total = F[t, at(x * span + g * 32, 32), :]
            for j in range(NX - 1):
                total = total + P1[j, rows, lanes].astype(F32)
            P1S[rows, lanes] = total.astype(BF16)

    loop(span // 32, sum_x)

    def send_z(j):
        to = lax.rem(z + j, NZ)
        remote(
            P1S.at[at(to * ROWS_A, ROWS_A), :], P2.at[at(z * ROWS_A, ROWS_A), :],
            p2_send, p2_recv, dev(rm, cm, x * NZ + to),
        ).start()

    loop(NZ, send_z)

    def edge_grad(q):
        cols = at(q * QW, QW)
        whole = G.at[:, cols]
        remote(whole, whole, ab_send.at[q], ab_recv.at[q], dev(rm, c, e)).wait_recv()
        TE[cols, :] = dot_tn(G[:, cols], GN[...]).astype(BF16)

        def store(j):
            k = q * KQ + j
            pltpu.make_async_copy(
                TE.at[at(k * ROWS_A, ROWS_A), :], ge_out.at[:, at(k * CHI, CHI)], out_sem
            ).start()

        loop(KQ, store)

    loop(QN, edge_grad)

    remote(P2, P2, p2_send, p2_recv, dev(rm, cm, e)).wait_recv()
    for t in range(CHI // LANE):
        lanes = slice(t * LANE, (t + 1) * LANE)
        total = P2[0:ROWS_A, lanes].astype(F32)
        for j in range(1, NZ):
            total = total + P2[j * ROWS_A:(j + 1) * ROWS_A, lanes].astype(F32)
        gc_out[:, lanes] = total.astype(BF16)

    ps_copy.wait_recv()
    row = lax.broadcasted_iota(jnp.int32, (ROWS_A, LANE), 0)
    lane = lax.broadcasted_iota(jnp.int32, (ROWS_A, LANE), 1)
    tile = vals[0:1, at((e // (LANE // ROWS_A)) * LANE, LANE)]
    mine = lane == row + lax.rem(e, LANE // ROWS_A) * ROWS_A
    value = jnp.sum(jnp.where(mine, jnp.broadcast_to(tile, (ROWS_A, LANE)), 0.0), axis=1, keepdims=True)
    grads = -0.5 * PSR[...] / value
    gv_out[...] = jnp.sum(jnp.where(lane == row, grads, 0.0), axis=0, keepdims=True)[:, :ROWS_A]

    ps_copy.wait_send()
    remote(CH, CHR, ch_send, ch_recv, dev(rp, c, e)).wait_send()
    remote(CR, CR, cn_send, cn_recv.at[0], dev(rp, cp, e)).wait_send()
    for q in range(QN):
        part = GFS.at[:, q * QW:(q + 1) * QW]
        remote(part, part, gf_send.at[q], gf_recv.at[q], dev(rp, c, e)).wait_send()
        part = AS.at[:, q * QW:(q + 1) * QW]
        remote(part, part, ab_send.at[q], ab_recv.at[q], dev(rm, c, e)).wait_send()
    remote(P1, P1, p1_send, p1_recv, dev(r, c, e)).wait_send()
    remote(P1S, P1S, p2_send, p2_recv, dev(rm, cm, e)).wait_send()
    gh_copy.wait()
    pltpu.make_async_copy(TE, TE, out_sem).wait()


def absorb_backward(sizes, corner, te, lh, cot, vals, par):
    nr, nc, ne = sizes
    hbm = pl.BlockSpec(memory_space=pltpu.HBM)
    free = pl.BlockSpec(memory_space=pl.ANY)
    vmem = pl.BlockSpec(memory_space=pltpu.VMEM)
    dma = pltpu.SemaphoreType.DMA
    square = pltpu.VMEM((CHI, CHI), BF16)
    tiles = pltpu.VMEM((CHI // LANE, CHI, LANE), F32)
    charges = pltpu.VMEM((8, CHI), jnp.int32)
    scratch = [
        square, square, pltpu.VMEM((ROWS_A, CHI * HALF), BF16), square, charges, charges,
        pltpu.VMEM((CHI, CHI), F32),
        square, square, square, square, square, square, square,
        pltpu.VMEM((GRP * ROWS_A, LANE), F32), tiles, tiles, square,
        pltpu.VMEM((NX - 1, CHI // NX, CHI), BF16), pltpu.VMEM((CHI // NX, CHI), BF16),
        pltpu.VMEM((NZ * ROWS_A, CHI), BF16),
        pltpu.VMEM((ROWS_A, LANE), F32), pltpu.VMEM((ROWS_A, LANE), F32), pltpu.VMEM((ROWS_A, LANE), F32),
        dma((QN,)), dma((QN,)), dma, dma, dma, dma((NBLK,)), dma, dma,
        dma((QN,)), dma((QN,)), dma((QN,)), dma((QN,)), dma, dma, dma, dma, dma, dma,
    ]
    return pl.pallas_call(
        functools.partial(kernel, nr, nc, ne),
        out_shape=(
            jax.ShapeDtypeStruct((ROWS_A, CHI), BF16),
            jax.ShapeDtypeStruct((ROWS_A, HALF * CHI), BF16),
            jax.ShapeDtypeStruct((ROWS_A, CHI * HALF), BF16),
            jax.ShapeDtypeStruct((1, ROWS_A), F32),
        ),
        in_specs=[hbm, hbm, hbm, hbm, vmem, vmem],
        out_specs=(vmem, free, free, vmem),
        scratch_shapes=scratch,
        compiler_params=pltpu.CompilerParams(
            collective_id=0, has_side_effects=True, vmem_limit_bytes=54 * 1024 * 1024
        ),
    )(corner, te, lh, cot, vals, par)


def shards(sizes, corner, top_edge, half_system, values, cotangent, parity):
    gc, ge, gh, gv = absorb_backward(
        sizes, corner[0, 0], top_edge[0, 0], half_system[0, 0], cotangent[0, 0], values[0], parity[0, 0]
    )
    return gc[None, None], ge[None, None], gh[None, None], gv[None]


def solution(mesh):
    placed = (
        P("row", "col", None, None),
        P("row", "col", "env", None),
        P("row", "col", "env", None),
        P("row", "col", None),
        P("row", "col", None, None),
        P("row", "col", None, None),
    )
    sizes = (mesh.shape["row"], mesh.shape["col"], mesh.shape["env"])
    return jax.shard_map(
        functools.partial(shards, sizes),
        mesh=mesh,
        in_specs=placed,
        out_specs=(
            P("row", "col", "env", None),
            P("row", "col", "env", None),
            P("row", "col", "env", None),
            P("row", "col", "env"),
        ),
        check_vma=False,
    )
```

```python
import functools

import jax
import jax.numpy as jnp
from jax import lax
from jax.experimental import pallas as pl
from jax.experimental.pallas import tpu as pltpu
from jax.sharding import PartitionSpec as P

CHI = 1024
HALF = 32
BLK = 128
NBLK = CHI // BLK
LANE = 128
SUB = 4
GRP = CHI // SUB
NX, NZ = 4, 8
ROWS_A = 32
QN = 4
QW = CHI // QN
KQ = HALF // QN
MESH = pl.DeviceIdType.MESH
F32 = jnp.float32
BF16 = jnp.bfloat16


def tile_mix(tiles):
    lane = lax.broadcasted_iota(jnp.int32, tiles[0].shape, 1)
    low = lane < 64
    even = (lane // 32) % 2 == 0
    roll = lambda t, by: pltpu.roll(t, by, 1)
    x0, x1, x2, x3 = tiles
    y0 = jnp.where(low, x0, roll(x2, 64))
    y2 = jnp.where(low, roll(x0, 64), x2)
    y1 = jnp.where(low, x1, roll(x3, 64))
    y3 = jnp.where(low, roll(x1, 64), x3)
    z0 = jnp.where(even, y0, roll(y1, 32))
    z1 = jnp.where(even, roll(y0, 96), y1)
    z2 = jnp.where(even, y2, roll(y3, 32))
    z3 = jnp.where(even, roll(y2, 96), y3)
    return z0, z1, z2, z3


def dot_nn(a, b):
    return lax.dot_general(a, b, (((1,), (0,)), ((), ())), preferred_element_type=F32)


def dot_nt(a, b):
    return lax.dot_general(a, b, (((1,), (1,)), ((), ())), preferred_element_type=F32)


def dot_tn(a, b):
    return lax.dot_general(a, b, (((0,), (0,)), ((), ())), preferred_element_type=F32)


def at(start, size):
    return pl.ds(pl.multiple_of(start, size), size)


def loop(n, body):
    lax.fori_loop(0, n, lambda i, c: (body(i), c)[1], 0)


def kernel(
    nr, nc, ne,
    corner, te, lh, cot, vals, par,
    gc_out, ge_out, gh_out, gv_out,
    TE, GN, LHB, CR, CH, CHR, ACC, GFS, R, G, NCP, LHM, GFM, S, LM, F, P1, P1S, P2, PSA, PSS, PSR,
    te_sem, ct_sem, in_sem, cn_send, cn_recv, ch_send, ch_recv,
    gf_send, gf_recv, ab_send, ab_recv, p1_send, p1_recv, p2_send, p2_recv, ps_send, ps_recv,
):
    r, c, e = lax.axis_index("row"), lax.axis_index("col"), lax.axis_index("env")
    rp, rm = lax.rem(r + 1, nr), lax.rem(r + nr - 1, nr)
    cp, cm = lax.rem(c + 1, nc), lax.rem(c + nc - 1, nc)
    x, z = e // NZ, lax.rem(e, NZ)

    def dev(row, col, env):
        return {"row": row, "col": col, "env": env}

    def remote(src, dst, send, recv, where):
        return pltpu.make_async_remote_copy(
            src_ref=src, dst_ref=dst, send_sem=send, recv_sem=recv, device_id=where, device_id_type=MESH
        )

    AS, GCB = TE, CR

    barrier = pltpu.get_barrier_semaphore()

    def greet(where):
        pl.semaphore_signal(barrier, inc=1, device_id=where, device_id_type=MESH)

    def greet_env(s):
        greet(dev(rm, c, s))

    def greet_z(s):
        greet(dev(rp, cp, x * NZ + s))

    def greet_x(s):
        greet(dev(r, c, lax.rem(x + 1 + s, NX) * NZ + z))

    def turned(m):
        return lax.rem(e // (ne // QN) + m, QN)

    def load_cot(m):
        rows = at(turned(m) * QW, QW)
        pltpu.make_async_copy(cot.at[rows, :], GN.at[rows, :], ct_sem.at[turned(m)]).start()

    def load_edge(k):
        pltpu.make_async_copy(
            te.at[:, at(k * CHI, CHI)], TE.at[at(k * ROWS_A, ROWS_A), :], te_sem.at[k // KQ]
        ).start()

    loop(ne, greet_env)
    loop(NZ, greet_z)
    loop(NX - 1, greet_x)
    greet(dev(rm, cm, e))
    loop(1, load_cot)
    loop(KQ, load_edge)
    loop(QN - 1, lambda m: load_cot(m + 1))
    loop(HALF - KQ, lambda k: load_edge(k + KQ))
    lh_copy = pltpu.make_async_copy(lh, LHB, in_sem)
    lh_copy.start()

    for role in range(4):
        for g in range(NBLK):
            CH[role:role + 1, g * BLK:(g + 1) * BLK] = jnp.broadcast_to(par[role:role + 1, g:g + 1], (1, BLK))

    def weigh(m):
        rows = at(turned(m) * QW, QW)
        part = GN.at[rows, :]
        pltpu.make_async_copy(part, part, ct_sem.at[turned(m)]).wait()

        def block(g):
            rows = at(turned(m) * QW + g * BLK, BLK)
            weight = jnp.broadcast_to(lax.rsqrt(vals[0:1, rows]), (BLK, BLK)).T
            charge = CH[2:3, rows]
            for t in range(NBLK):
                lanes = slice(t * BLK, (t + 1) * BLK)
                keep = charge == CH[3:4, lanes]
                GN[rows, lanes] = jnp.where(keep, weight * GN[rows, lanes].astype(F32), 0.0).astype(BF16)

        loop(QW // BLK, block)

    odd = lax.rem(x, 2)
    first = [2 * odd, 6 - 2 * odd, 2 * odd + 1, 7 - 2 * odd]
    right, left = lax.rem(x + 1, NX), lax.rem(x + NX - 1, NX)
    near = jnp.where(odd == 0, right, left)
    far = jnp.where(odd == 0, left, right)

    def send_corner():
        for g in first:
            rows = at(g * BLK, BLK)
            remote(corner.at[rows, :], CR.at[rows, :], cn_send, cn_recv.at[g], dev(rp, cp, e)).start()

    def forward_corner():
        for n, g in enumerate(first):
            part = CR.at[at(g * BLK, BLK), :]
            to = dev(r, c, (near if n % 2 == 0 else far) * NZ + z)
            copy = remote(part, part, cn_send, cn_recv.at[g], to)
            copy.wait_recv()
            copy.start()

    def edge_rows(q, m):
        rows = at(turned(m) * QW, QW)
        cols = at(q * QW, QW)
        GFS[rows, cols] = dot_nt(GN[rows, :], TE[cols, :]).astype(BF16)

    def send_full(q, m):
        def send(j):
            s = turned(m) * (ne // QN) + lax.rem(e + j, ne // QN)
            remote(
                GFS.at[at(s * ROWS_A, ROWS_A), at(q * QW, QW)], R.at[at(e * ROWS_A, ROWS_A), at(q * QW, QW)],
                gf_send.at[q], gf_recv.at[q], dev(rp, c, s),
            ).start()

        loop(ne // QN, send)

    def edge_ready(q):
        whole = TE.at[at(q * QW, QW), :]
        pltpu.make_async_copy(whole, whole, te_sem.at[q]).wait()

    weigh(0)
    edge_ready(0)
    edge_rows(0, 0)
    pl.semaphore_wait(barrier, ne + NZ + NX)
    send_full(0, 0)
    remote(CH, CHR, ch_send, ch_recv, dev(rp, c, e)).start()
    send_corner()

    def edge_first(m):
        weigh(m + 1)
        edge_rows(0, m + 1)
        send_full(0, m + 1)

    loop(QN - 1, edge_first)

    def edge_chunk(q):
        edge_ready(q + 1)

        def part(m):
            edge_rows(q + 1, m)
            send_full(q + 1, m)

        loop(QN, part)

    loop(QN - 1, edge_chunk)

    lh_copy.wait()

    def spread(g):
        for u in range(8):
            S[at((g * 8 + u) * ROWS_A, ROWS_A), :] = LHB[:, at((g * 8 + u) * LANE, LANE)].astype(F32)

    loop(GRP // 8, spread)

    def turn(i):
        t = S[pl.ds(i, GRP, stride=ROWS_A), :].T
        for s in range(SUB):
            for h in range(GRP // LANE):
                LM[s * (GRP // LANE) + h, pl.ds(i, HALF, stride=ROWS_A), :] = t[
                    s * HALF:(s + 1) * HALF, h * LANE:(h + 1) * LANE]

    loop(ROWS_A, turn)

    def narrow(k):
        rows = at(k * ROWS_A, ROWS_A)
        for t in range(CHI // LANE):
            LHM[rows, t * LANE:(t + 1) * LANE] = LM[t, rows, :].astype(BF16)

    loop(HALF, narrow)
    forward_corner()

    def half_chunk(q):
        cols = at(q * QW, QW)
        whole = R.at[:, cols]
        remote(whole, whole, gf_send.at[q], gf_recv.at[q], dev(rp, c, e)).wait_recv()

        def regroup(d):
            for k2 in range(KQ // 4):
                lanes = at(q * QW + k2 * LANE, LANE)
                mixed = tile_mix([
                    R[at((d * 4 + d4) * ROWS_A, ROWS_A), lanes].astype(F32) for d4 in range(4)])
                for k4 in range(4):
                    GFM[at((q * KQ + k2 * 4 + k4) * ROWS_A, ROWS_A), at(d * LANE, LANE)] = mixed[k4].astype(BF16)

        loop(CHI // LANE, regroup)

        def add(s):
            rows = at(s * GRP, GRP)
            ACC[rows, :] = ACC[rows, :] + dot_tn(LHM[cols, rows], GFM[cols, :])

        loop(SUB, add)

    def clear(g):
        rows = at(g * 32, 32)
        ACC[rows, :] = jnp.zeros((32, CHI), F32)

    loop(CHI // 32, clear)
    loop(QN - 1, half_chunk)

    remote(CHR, CHR, ch_send, ch_recv, dev(rp, c, e)).wait_recv()

    def corner_rows(g):
        rows = at(g * BLK, BLK)

        @pl.when(jnp.logical_and(g // 2 != odd, g // 2 != 3 - odd))
        def _():
            part = CR.at[rows, :]
            remote(part, part, cn_send, cn_recv.at[g], dev(rp, cp, e)).wait_recv()

        charge = CHR[0:1, rows]
        for t in range(CHI // LANE):
            lanes = slice(t * LANE, (t + 1) * LANE)
            same = charge == CHR[1:2, lanes]
            F[t, rows, :] = jnp.where(same, CR[rows, lanes].astype(F32), 0.0)
            for s in range(SUB):
                NCP[at(s * GRP + g * (BLK // SUB), BLK // SUB), lanes] = F[
                    t, pl.ds(g * BLK + s, BLK // SUB, stride=SUB), :].astype(BF16)

    loop(NBLK, corner_rows)

    def absorb_chunk(q):
        cols = at(q * QW, QW)

        def columns_of(n):
            t = dot_nn(LHM[cols, :], NCP[:, at(n * 256, 256)])
            for k2 in range(KQ // 4):
                for d2 in range(2):
                    mixed = tile_mix([
                        t[(k2 * 4 + k4) * ROWS_A:(k2 * 4 + k4 + 1) * ROWS_A, d2 * LANE:(d2 + 1) * LANE]
                        for k4 in range(4)])
                    for d4 in range(4):
                        AS[at(((n * 2 + d2) * 4 + d4) * ROWS_A, ROWS_A), at(q * QW + k2 * LANE, LANE)] = (
                            mixed[d4].astype(BF16))

        loop(CHI // 256, columns_of)

    def absorb_send(q):
        cols = at(q * QW, QW)

        def send(j):
            s = lax.rem(e + j, ne)
            remote(
                AS.at[at(s * ROWS_A, ROWS_A), cols], G.at[at(e * ROWS_A, ROWS_A), cols],
                ab_send.at[q], ab_recv.at[q], dev(rm, c, s),
            ).start()

        loop(ne, send)

    absorb_chunk(0)
    absorb_send(0)

    half_chunk(QN - 1)

    def corner_part(s):
        def block(g):
            for h in range(CHI // LANE):
                lanes = slice(h * LANE, (h + 1) * LANE)
                same = CHR[0:1, at(g * BLK, BLK)] == CHR[1:2, lanes]
                part = ACC[at(s * GRP + g * (BLK // SUB), BLK // SUB), lanes]
                F[h, pl.ds(g * BLK + s, BLK // SUB, stride=SUB), :] = jnp.where(same, part, 0.0)

        loop(NBLK, block)

    loop(SUB, corner_part)

    remote(CR, CR, cn_send, cn_recv.at[0], dev(rp, cp, e)).wait_send()

    def corner_narrow(g):
        rows = at(g * 32, 32)
        for t in range(CHI // LANE):
            GCB[rows, t * LANE:(t + 1) * LANE] = F[t, rows, :].astype(BF16)

    loop(CHI // 32, corner_narrow)
    span = CHI // NX

    def send_x(j):
        to = lax.rem(x + 1 + j, NX)
        remote(
            GCB.at[at(to * span, span), :], P1.at[j], p1_send, p1_recv, dev(r, c, to * NZ + z)
        ).start()

    loop(NX - 1, send_x)

    def absorb_more(q):
        absorb_chunk(q + 1)
        absorb_send(q + 1)

    loop(QN - 1, absorb_more)

    def pair(d):
        rows = at(d * ROWS_A, ROWS_A)
        total = PSA[...]
        for t in range(CHI // LANE):
            lanes = slice(t * LANE, (t + 1) * LANE)
            total = total + R[rows, lanes].astype(F32) * AS[rows, lanes].astype(F32)
        PSA[...] = total

    PSA[...] = jnp.zeros_like(PSA)
    loop(ne, pair)
    PSS[...] = jnp.broadcast_to(jnp.sum(PSA[...], axis=1, keepdims=True), (ROWS_A, LANE))
    ps_copy = remote(PSS, PSR, ps_send, ps_recv, dev(rm, c, e))
    ps_copy.start()

    def half_rows(q):
        cols = at(q * QW, QW)

        def half_cols(n):
            t = dot_nt(GFM[cols, :], NCP[at(n * 256, 256), :])
            for h in range(2):
                LM[n * 2 + h, cols, :] = t[:, h * LANE:(h + 1) * LANE]

        loop(CHI // 256, half_cols)

    loop(QN, half_rows)

    def turn_back(i):
        t = jnp.concatenate([
            jnp.concatenate([
                LM[s * (GRP // LANE) + h, pl.ds(i, HALF, stride=ROWS_A), :] for h in range(GRP // LANE)
            ], axis=1) for s in range(SUB)], axis=0)
        S[pl.ds(i, GRP, stride=ROWS_A), :] = t.T

    loop(ROWS_A, turn_back)

    def gather(g):
        for u in range(8):
            gh_out[:, at((g * 8 + u) * LANE, LANE)] = S[at((g * 8 + u) * ROWS_A, ROWS_A), :].astype(BF16)

    loop(GRP // 8, gather)

    remote(P1, P1, p1_send, p1_recv, dev(r, c, e)).wait_recv()

    def sum_x(g):
        rows = at(g * 32, 32)
        for t in range(CHI // LANE):
            lanes = slice(t * LANE, (t + 1) * LANE)
            total = F[t, at(x * span + g * 32, 32), :]
            for j in range(NX - 1):
                total = total + P1[j, rows, lanes].astype(F32)
            P1S[rows, lanes] = total.astype(BF16)

    loop(span // 32, sum_x)

    def send_z(j):
        to = lax.rem(z + j, NZ)
        remote(
            P1S.at[at(to * ROWS_A, ROWS_A), :], P2.at[at(z * ROWS_A, ROWS_A), :],
            p2_send, p2_recv, dev(rm, cm, x * NZ + to),
        ).start()

    loop(NZ, send_z)

    def edge_grad(q):
        cols = at(q * QW, QW)
        whole = G.at[:, cols]
        remote(whole, whole, ab_send.at[q], ab_recv.at[q], dev(rm, c, e)).wait_recv()
        ge_out[cols, :] = dot_tn(G[:, cols], GN[...]).astype(BF16)

    loop(QN, edge_grad)

    remote(P2, P2, p2_send, p2_recv, dev(rm, cm, e)).wait_recv()
    for t in range(CHI // LANE):
        lanes = slice(t * LANE, (t + 1) * LANE)
        total = P2[0:ROWS_A, lanes].astype(F32)
        for j in range(1, NZ):
            total = total + P2[j * ROWS_A:(j + 1) * ROWS_A, lanes].astype(F32)
        gc_out[:, lanes] = total.astype(BF16)

    ps_copy.wait_recv()
    row = lax.broadcasted_iota(jnp.int32, (ROWS_A, LANE), 0)
    lane = lax.broadcasted_iota(jnp.int32, (ROWS_A, LANE), 1)
    tile = vals[0:1, at((e // (LANE // ROWS_A)) * LANE, LANE)]
    mine = lane == row + lax.rem(e, LANE // ROWS_A) * ROWS_A
    value = jnp.sum(jnp.where(mine, jnp.broadcast_to(tile, (ROWS_A, LANE)), 0.0), axis=1, keepdims=True)
    grads = -0.5 * PSR[...] / value
    gv_out[...] = jnp.sum(jnp.where(lane == row, grads, 0.0), axis=0, keepdims=True)[:, :ROWS_A]

    ps_copy.wait_send()
    remote(CH, CHR, ch_send, ch_recv, dev(rp, c, e)).wait_send()
    for q in range(QN):
        part = GFS.at[:, q * QW:(q + 1) * QW]
        remote(part, part, gf_send.at[q], gf_recv.at[q], dev(rp, c, e)).wait_send()
        part = AS.at[:, q * QW:(q + 1) * QW]
        remote(part, part, ab_send.at[q], ab_recv.at[q], dev(rm, c, e)).wait_send()
    remote(P1, P1, p1_send, p1_recv, dev(r, c, e)).wait_send()
    remote(P1S, P1S, p2_send, p2_recv, dev(rm, cm, e)).wait_send()


def absorb_backward(sizes, corner, te, lh, cot, vals, par):
    nr, nc, ne = sizes
    hbm = pl.BlockSpec(memory_space=pltpu.HBM)
    vmem = pl.BlockSpec(memory_space=pltpu.VMEM)
    dma = pltpu.SemaphoreType.DMA
    square = pltpu.VMEM((CHI, CHI), BF16)
    tiles = pltpu.VMEM((CHI // LANE, CHI, LANE), F32)
    charges = pltpu.VMEM((8, CHI), jnp.int32)
    scratch = [
        square, square, pltpu.VMEM((ROWS_A, CHI * HALF), BF16), square, charges, charges,
        pltpu.VMEM((CHI, CHI), F32),
        square, square, square, square, square, square,
        pltpu.VMEM((GRP * ROWS_A, LANE), F32), tiles, tiles,
        pltpu.VMEM((NX - 1, CHI // NX, CHI), BF16), pltpu.VMEM((CHI // NX, CHI), BF16),
        pltpu.VMEM((NZ * ROWS_A, CHI), BF16),
        pltpu.VMEM((ROWS_A, LANE), F32), pltpu.VMEM((ROWS_A, LANE), F32), pltpu.VMEM((ROWS_A, LANE), F32),
        dma((QN,)), dma((QN,)), dma, dma, dma((NBLK,)), dma, dma,
        dma((QN,)), dma((QN,)), dma((QN,)), dma((QN,)), dma, dma, dma, dma, dma, dma,
    ]
    return pl.pallas_call(
        functools.partial(kernel, nr, nc, ne),
        out_shape=(
            pltpu.VMEM((ROWS_A, CHI), BF16),
            pltpu.VMEM((CHI, CHI), BF16),
            pltpu.VMEM((ROWS_A, CHI * HALF), BF16),
            pltpu.VMEM((1, ROWS_A), F32),
        ),
        in_specs=[hbm, hbm, hbm, hbm, vmem, vmem],
        out_specs=(vmem, vmem, vmem, vmem),
        scratch_shapes=scratch,
        compiler_params=pltpu.CompilerParams(
            collective_id=0, has_side_effects=True, vmem_limit_bytes=58 * 1024 * 1024
        ),
    )(corner, te, lh, cot, vals, par)


def store_kernel(gc, ge, gh, gv, gc_out, ge_out, gh_out, gv_out, sem):
    def edge(k):
        return pltpu.make_async_copy(
            ge.at[at(k * ROWS_A, ROWS_A), :], ge_out.at[:, at(k * CHI, CHI)], sem.at[0])

    loop(HALF, lambda k: edge(k).start())
    rest = [
        pltpu.make_async_copy(src, dst, sem.at[1 + n])
        for n, (src, dst) in enumerate(((gh, gh_out), (gc, gc_out), (gv, gv_out)))]
    for copy in rest:
        copy.start()
    pltpu.make_async_copy(ge, ge, sem.at[0]).wait()
    for copy in rest:
        copy.wait()


def store(gc, ge, gh, gv):
    vmem = pl.BlockSpec(memory_space=pltpu.VMEM)
    hbm = pl.BlockSpec(memory_space=pltpu.HBM)
    return pl.pallas_call(
        store_kernel,
        out_shape=(
            jax.ShapeDtypeStruct((ROWS_A, CHI), BF16),
            jax.ShapeDtypeStruct((ROWS_A, HALF * CHI), BF16),
            jax.ShapeDtypeStruct((ROWS_A, CHI * HALF), BF16),
            jax.ShapeDtypeStruct((1, ROWS_A), F32),
        ),
        in_specs=[vmem] * 4,
        out_specs=(hbm,) * 4,
        scratch_shapes=[pltpu.SemaphoreType.DMA((4,))],
        compiler_params=pltpu.CompilerParams(vmem_limit_bytes=16 * 1024 * 1024),
    )(*(pltpu.with_memory_space_constraint(t, pltpu.VMEM) for t in (gc, ge, gh, gv)))


def shards(sizes, corner, top_edge, half_system, values, cotangent, parity):
    gc, ge, gh, gv = store(*absorb_backward(
        sizes, corner[0, 0], top_edge[0, 0], half_system[0, 0], cotangent[0, 0], values[0], parity[0, 0]
    ))
    return gc[None, None], ge[None, None], gh[None, None], gv[None]


def solution(mesh):
    placed = (
        P("row", "col", None, None),
        P("row", "col", "env", None),
        P("row", "col", "env", None),
        P("row", "col", None),
        P("row", "col", None, None),
        P("row", "col", None, None),
    )
    sizes = (mesh.shape["row"], mesh.shape["col"], mesh.shape["env"])
    return jax.shard_map(
        functools.partial(shards, sizes),
        mesh=mesh,
        in_specs=placed,
        out_specs=(
            P("row", "col", "env", None),
            P("row", "col", "env", None),
            P("row", "col", "env", None),
            P("row", "col", "env"),
        ),
        check_vma=False,
    )
```

```python
import functools

import jax
import jax.numpy as jnp
from jax import lax
from jax.experimental import pallas as pl
from jax.experimental.pallas import tpu as pltpu
from jax.sharding import PartitionSpec as P

CHI = 1024
HALF = 32
BLK = 128
NBLK = CHI // BLK
LANE = 128
SUB = 4
GRP = CHI // SUB
NX, NZ = 4, 8
ROWS_A = 32
QN = 4
QW = CHI // QN
KQ = HALF // QN
MESH = pl.DeviceIdType.MESH
F32 = jnp.float32
BF16 = jnp.bfloat16


def tile_mix(tiles):
    lane = lax.broadcasted_iota(jnp.int32, tiles[0].shape, 1)
    low = lane < 64
    even = (lane // 32) % 2 == 0
    roll = lambda t, by: pltpu.roll(t, by, 1)
    x0, x1, x2, x3 = tiles
    y0 = jnp.where(low, x0, roll(x2, 64))
    y2 = jnp.where(low, roll(x0, 64), x2)
    y1 = jnp.where(low, x1, roll(x3, 64))
    y3 = jnp.where(low, roll(x1, 64), x3)
    z0 = jnp.where(even, y0, roll(y1, 32))
    z1 = jnp.where(even, roll(y0, 96), y1)
    z2 = jnp.where(even, y2, roll(y3, 32))
    z3 = jnp.where(even, roll(y2, 96), y3)
    return z0, z1, z2, z3


def dot_nn(a, b):
    return lax.dot_general(a, b, (((1,), (0,)), ((), ())), preferred_element_type=F32)


def dot_nt(a, b):
    return lax.dot_general(a, b, (((1,), (1,)), ((), ())), preferred_element_type=F32)


def dot_tn(a, b):
    return lax.dot_general(a, b, (((0,), (0,)), ((), ())), preferred_element_type=F32)


def at(start, size):
    return pl.ds(pl.multiple_of(start, size), size)


def loop(n, body):
    lax.fori_loop(0, n, lambda i, c: (body(i), c)[1], 0)


def kernel(
    nr, nc, ne,
    corner, te, lh, cot, vals, par,
    gc_out, ge_out, gh_out, gv_out,
    TE, GN, LHB, CR, CH, CHR, ACC, GFS, R, G, NCP, LHM, GFM, S, LM, F, P1, P1S, PT, PU, P2, PSA, PSS, PSR,
    te_sem, ct_sem, in_sem, cn_send, cn_recv, ch_send, ch_recv,
    gf_send, gf_recv, ab_send, ab_recv, p1_send, p1_recv, pt_send, pt_recv, p2_send, p2_recv, ps_send, ps_recv,
):
    r, c, e = lax.axis_index("row"), lax.axis_index("col"), lax.axis_index("env")
    rp, rm = lax.rem(r + 1, nr), lax.rem(r + nr - 1, nr)
    cp, cm = lax.rem(c + 1, nc), lax.rem(c + nc - 1, nc)
    x, z = e // NZ, lax.rem(e, NZ)

    def dev(row, col, env):
        return {"row": row, "col": col, "env": env}

    def remote(src, dst, send, recv, where):
        return pltpu.make_async_remote_copy(
            src_ref=src, dst_ref=dst, send_sem=send, recv_sem=recv, device_id=where, device_id_type=MESH
        )

    AS, GCB = TE, CR

    barrier = pltpu.get_barrier_semaphore()

    def greet(where):
        pl.semaphore_signal(barrier, inc=1, device_id=where, device_id_type=MESH)

    def greet_env(s):
        greet(dev(rm, c, s))

    def greet_z(s):
        greet(dev(rp, cp, x * NZ + s))

    def greet_x(s):
        greet(dev(r, c, lax.rem(x + 1 + s, NX) * NZ + z))

    def turned(m):
        return lax.rem(e // (ne // QN) + m, QN)

    def load_cot(m):
        rows = at(turned(m) * QW, QW)
        pltpu.make_async_copy(cot.at[rows, :], GN.at[rows, :], ct_sem.at[turned(m)]).start()

    def load_edge(k):
        pltpu.make_async_copy(
            te.at[:, at(k * CHI, CHI)], TE.at[at(k * ROWS_A, ROWS_A), :], te_sem.at[k // KQ]
        ).start()

    loop(ne, greet_env)
    loop(NZ, greet_z)
    loop(NX - 1, greet_x)
    greet(dev(rm, cm, e))
    greet(dev(r, c, x * NZ + lax.rem(z + 1, NZ)))
    greet(dev(r, c, x * NZ + lax.rem(z + NZ - 1, NZ)))
    loop(1, load_cot)
    loop(KQ, load_edge)
    loop(QN - 1, lambda m: load_cot(m + 1))
    loop(HALF - KQ, lambda k: load_edge(k + KQ))
    lh_copy = pltpu.make_async_copy(lh, LHB, in_sem)
    lh_copy.start()

    for role in range(4):
        for g in range(NBLK):
            CH[role:role + 1, g * BLK:(g + 1) * BLK] = jnp.broadcast_to(par[role:role + 1, g:g + 1], (1, BLK))

    def weigh(m):
        rows = at(turned(m) * QW, QW)
        part = GN.at[rows, :]
        pltpu.make_async_copy(part, part, ct_sem.at[turned(m)]).wait()

        def block(g):
            rows = at(turned(m) * QW + g * BLK, BLK)
            weight = jnp.broadcast_to(lax.rsqrt(vals[0:1, rows]), (BLK, BLK)).T
            charge = CH[2:3, rows]
            for t in range(NBLK):
                lanes = slice(t * BLK, (t + 1) * BLK)
                keep = charge == CH[3:4, lanes]
                GN[rows, lanes] = jnp.where(keep, weight * GN[rows, lanes].astype(F32), 0.0).astype(BF16)

        loop(QW // BLK, block)

    odd = lax.rem(x, 2)
    first = [2 * odd, 6 - 2 * odd, 2 * odd + 1, 7 - 2 * odd]
    right, left = lax.rem(x + 1, NX), lax.rem(x + NX - 1, NX)
    near = jnp.where(odd == 0, right, left)
    far = jnp.where(odd == 0, left, right)

    def send_corner():
        for g in first:
            rows = at(g * BLK, BLK)
            remote(corner.at[rows, :], CR.at[rows, :], cn_send, cn_recv.at[g], dev(rp, cp, e)).start()

    def forward_corner():
        for n, g in enumerate(first):
            part = CR.at[at(g * BLK, BLK), :]
            to = dev(r, c, (near if n % 2 == 0 else far) * NZ + z)
            copy = remote(part, part, cn_send, cn_recv.at[g], to)
            copy.wait_recv()
            copy.start()

    def edge_rows(q, m):
        rows = at(turned(m) * QW, QW)
        cols = at(q * QW, QW)
        GFS[rows, cols] = dot_nt(GN[rows, :], TE[cols, :]).astype(BF16)

    def send_full(q, m):
        def send(j):
            s = turned(m) * (ne // QN) + lax.rem(e + j, ne // QN)
            remote(
                GFS.at[at(s * ROWS_A, ROWS_A), at(q * QW, QW)], R.at[at(e * ROWS_A, ROWS_A), at(q * QW, QW)],
                gf_send.at[q], gf_recv.at[q], dev(rp, c, s),
            ).start()

        loop(ne // QN, send)

    def edge_ready(q):
        whole = TE.at[at(q * QW, QW), :]
        pltpu.make_async_copy(whole, whole, te_sem.at[q]).wait()

    weigh(0)
    edge_ready(0)
    edge_rows(0, 0)
    pl.semaphore_wait(barrier, ne + NZ + NX + 2)
    send_full(0, 0)
    remote(CH, CHR, ch_send, ch_recv, dev(rp, c, e)).start()
    send_corner()

    def edge_first(m):
        weigh(m + 1)
        edge_rows(0, m + 1)
        send_full(0, m + 1)

    loop(QN - 1, edge_first)

    def edge_chunk(q):
        edge_ready(q + 1)

        def part(m):
            edge_rows(q + 1, m)
            send_full(q + 1, m)

        loop(QN, part)

    loop(QN - 1, edge_chunk)

    lh_copy.wait()

    def spread(g):
        for u in range(8):
            S[at((g * 8 + u) * ROWS_A, ROWS_A), :] = LHB[:, at((g * 8 + u) * LANE, LANE)].astype(F32)

    loop(GRP // 8, spread)

    def turn(i):
        t = S[pl.ds(i, GRP, stride=ROWS_A), :].T
        for s in range(SUB):
            for h in range(GRP // LANE):
                LM[s * (GRP // LANE) + h, pl.ds(i, HALF, stride=ROWS_A), :] = t[
                    s * HALF:(s + 1) * HALF, h * LANE:(h + 1) * LANE]

    loop(ROWS_A, turn)

    def narrow(k):
        rows = at(k * ROWS_A, ROWS_A)
        for t in range(CHI // LANE):
            LHM[rows, t * LANE:(t + 1) * LANE] = LM[t, rows, :].astype(BF16)

    loop(HALF, narrow)
    forward_corner()

    def half_chunk(q):
        cols = at(q * QW, QW)
        whole = R.at[:, cols]
        remote(whole, whole, gf_send.at[q], gf_recv.at[q], dev(rp, c, e)).wait_recv()

        def regroup(d):
            for k2 in range(KQ // 4):
                lanes = at(q * QW + k2 * LANE, LANE)
                mixed = tile_mix([
                    R[at((d * 4 + d4) * ROWS_A, ROWS_A), lanes].astype(F32) for d4 in range(4)])
                for k4 in range(4):
                    GFM[at((q * KQ + k2 * 4 + k4) * ROWS_A, ROWS_A), at(d * LANE, LANE)] = mixed[k4].astype(BF16)

        loop(CHI // LANE, regroup)

        def add(s):
            rows = at(s * GRP, GRP)
            ACC[rows, :] = ACC[rows, :] + dot_tn(LHM[cols, rows], GFM[cols, :])

        loop(SUB, add)

    def clear(g):
        rows = at(g * 32, 32)
        ACC[rows, :] = jnp.zeros((32, CHI), F32)

    loop(CHI // 32, clear)
    loop(QN - 1, half_chunk)

    remote(CHR, CHR, ch_send, ch_recv, dev(rp, c, e)).wait_recv()

    def corner_rows(g):
        rows = at(g * BLK, BLK)

        @pl.when(jnp.logical_and(g // 2 != odd, g // 2 != 3 - odd))
        def _():
            part = CR.at[rows, :]
            remote(part, part, cn_send, cn_recv.at[g], dev(rp, cp, e)).wait_recv()

        charge = CHR[0:1, rows]
        for t in range(CHI // LANE):
            lanes = slice(t * LANE, (t + 1) * LANE)
            same = charge == CHR[1:2, lanes]
            F[t, rows, :] = jnp.where(same, CR[rows, lanes].astype(F32), 0.0)
            for s in range(SUB):
                NCP[at(s * GRP + g * (BLK // SUB), BLK // SUB), lanes] = F[
                    t, pl.ds(g * BLK + s, BLK // SUB, stride=SUB), :].astype(BF16)

    loop(NBLK, corner_rows)

    def absorb_chunk(q):
        cols = at(q * QW, QW)

        def columns_of(n):
            t = dot_nn(LHM[cols, :], NCP[:, at(n * 256, 256)])
            for k2 in range(KQ // 4):
                for d2 in range(2):
                    mixed = tile_mix([
                        t[(k2 * 4 + k4) * ROWS_A:(k2 * 4 + k4 + 1) * ROWS_A, d2 * LANE:(d2 + 1) * LANE]
                        for k4 in range(4)])
                    for d4 in range(4):
                        AS[at(((n * 2 + d2) * 4 + d4) * ROWS_A, ROWS_A), at(q * QW + k2 * LANE, LANE)] = (
                            mixed[d4].astype(BF16))

        loop(CHI // 256, columns_of)

    def absorb_to(q, s):
        cols = at(q * QW, QW)
        remote(
            AS.at[at(s * ROWS_A, ROWS_A), cols], G.at[at(e * ROWS_A, ROWS_A), cols],
            ab_send.at[q], ab_recv.at[q], dev(rm, c, s),
        ).start()

    def absorb_same_x(q):
        loop(NZ, lambda j: absorb_to(q, x * NZ + lax.rem(z + j, NZ)))

    def absorb_other_x(q):
        loop(ne - NZ, lambda j: absorb_to(q, lax.rem(x + 1 + j // NZ, NX) * NZ + lax.rem(z + j, NZ)))

    absorb_chunk(0)
    absorb_other_x(0)
    absorb_same_x(0)

    half_chunk(QN - 1)

    def corner_part(s):
        def block(g):
            for h in range(CHI // LANE):
                lanes = slice(h * LANE, (h + 1) * LANE)
                same = CHR[0:1, at(g * BLK, BLK)] == CHR[1:2, lanes]
                part = ACC[at(s * GRP + g * (BLK // SUB), BLK // SUB), lanes]
                F[h, pl.ds(g * BLK + s, BLK // SUB, stride=SUB), :] = jnp.where(same, part, 0.0)

        loop(NBLK, block)

    loop(SUB, corner_part)

    remote(CR, CR, cn_send, cn_recv.at[0], dev(rp, cp, e)).wait_send()

    def corner_narrow(g):
        rows = at(g * 32, 32)
        for t in range(CHI // LANE):
            GCB[rows, t * LANE:(t + 1) * LANE] = F[t, rows, :].astype(BF16)

    loop(CHI // 32, corner_narrow)
    span = CHI // NX

    def send_x(j):
        to = lax.rem(x + 1 + j, NX)
        remote(
            GCB.at[at(to * span, span), :], P1.at[j], p1_send, p1_recv, dev(r, c, to * NZ + z)
        ).start()

    loop(NX - 1, send_x)

    def absorb_more(q):
        absorb_chunk(q + 1)
        absorb_same_x(q + 1)

    loop(QN - 1, absorb_more)
    loop(QN - 1, lambda q: absorb_other_x(q + 1))

    def pair(d):
        rows = at(d * ROWS_A, ROWS_A)
        total = PSA[...]
        for t in range(CHI // LANE):
            lanes = slice(t * LANE, (t + 1) * LANE)
            total = total + R[rows, lanes].astype(F32) * AS[rows, lanes].astype(F32)
        PSA[...] = total

    PSA[...] = jnp.zeros_like(PSA)
    loop(ne, pair)
    PSS[...] = jnp.broadcast_to(jnp.sum(PSA[...], axis=1, keepdims=True), (ROWS_A, LANE))
    ps_copy = remote(PSS, PSR, ps_send, ps_recv, dev(rm, c, e))
    ps_copy.start()

    def half_rows(q):
        cols = at(q * QW, QW)

        def half_cols(n):
            t = dot_nt(GFM[cols, :], NCP[at(n * 256, 256), :])
            for h in range(2):
                LM[n * 2 + h, cols, :] = t[:, h * LANE:(h + 1) * LANE]

        loop(CHI // 256, half_cols)

    loop(QN, half_rows)

    def turn_back(i):
        t = jnp.concatenate([
            jnp.concatenate([
                LM[s * (GRP // LANE) + h, pl.ds(i, HALF, stride=ROWS_A), :] for h in range(GRP // LANE)
            ], axis=1) for s in range(SUB)], axis=0)
        S[pl.ds(i, GRP, stride=ROWS_A), :] = t.T

    loop(ROWS_A, turn_back)

    def gather(g):
        for u in range(8):
            gh_out[:, at((g * 8 + u) * LANE, LANE)] = S[at((g * 8 + u) * ROWS_A, ROWS_A), :].astype(BF16)

    loop(GRP // 8, gather)

    remote(P1, P1, p1_send, p1_recv, dev(r, c, e)).wait_recv()

    def sum_x(g):
        rows = at(g * 32, 32)
        for t in range(CHI // LANE):
            lanes = slice(t * LANE, (t + 1) * LANE)
            mine = at(x * span + g * 32, 32)
            total = F[t, mine, :]
            for j in range(NX - 1):
                total = total + P1[j, rows, lanes].astype(F32)
            F[t, mine, :] = total
            P1S[rows, lanes] = total.astype(BF16)

    loop(span // 32, sum_x)

    wide = CHI // 2
    parts = [(h, t) for h in range(2) for t in range(NZ // 2)]
    sign = [2 * lax.rem(z, 2) - 1, 1 - 2 * lax.rem(z, 2)]

    def owner(h, t):
        return lax.rem(z + sign[h] * t + NZ, NZ)

    for h, t in parts:
        remote(
            P1S.at[at(owner(h, -1 - t) * ROWS_A, ROWS_A), h * wide:(h + 1) * wide],
            PT.at[(h * 4 + t) * ROWS_A:(h * 4 + t + 1) * ROWS_A, :],
            pt_send, pt_recv, dev(r, c, x * NZ + owner(h, -1)),
        ).start()

    def edge_grad(q):
        cols = at(q * QW, QW)
        whole = G.at[:, cols]
        remote(whole, whole, ab_send.at[q], ab_recv.at[q], dev(rm, c, e)).wait_recv()
        ge_out[cols, :] = dot_tn(G[:, cols], GN[...]).astype(BF16)

    edge_grad(0)
    remote(PT, PT, pt_send, pt_recv, dev(r, c, e)).wait_recv()
    for h, t in parts:
        rows = slice((h * 4 + t) * ROWS_A, (h * 4 + t + 1) * ROWS_A)
        mine = at(x * span + owner(h, t) * ROWS_A, ROWS_A)
        for n in range(wide // LANE):
            lanes = slice(n * LANE, (n + 1) * LANE)
            PU[rows, lanes] = (F[h * (wide // LANE) + n, mine, :] + PT[rows, lanes].astype(F32)).astype(BF16)
        remote(
            PU.at[rows, :], P2.at[t * ROWS_A:(t + 1) * ROWS_A, h * wide:(h + 1) * wide],
            p2_send, p2_recv, dev(rm, cm, x * NZ + owner(h, t)),
        ).start()

    loop(QN - 1, lambda q: edge_grad(q + 1))

    remote(P2, P2, p2_send, p2_recv, dev(rm, cm, e)).wait_recv()
    for t in range(CHI // LANE):
        lanes = slice(t * LANE, (t + 1) * LANE)
        total = P2[0:ROWS_A, lanes].astype(F32)
        for j in range(1, NZ // 2):
            total = total + P2[j * ROWS_A:(j + 1) * ROWS_A, lanes].astype(F32)
        gc_out[:, lanes] = total.astype(BF16)

    ps_copy.wait_recv()
    row = lax.broadcasted_iota(jnp.int32, (ROWS_A, LANE), 0)
    lane = lax.broadcasted_iota(jnp.int32, (ROWS_A, LANE), 1)
    tile = vals[0:1, at((e // (LANE // ROWS_A)) * LANE, LANE)]
    mine = lane == row + lax.rem(e, LANE // ROWS_A) * ROWS_A
    value = jnp.sum(jnp.where(mine, jnp.broadcast_to(tile, (ROWS_A, LANE)), 0.0), axis=1, keepdims=True)
    grads = -0.5 * PSR[...] / value
    gv_out[...] = jnp.sum(jnp.where(lane == row, grads, 0.0), axis=0, keepdims=True)[:, :ROWS_A]

    ps_copy.wait_send()
    remote(CH, CHR, ch_send, ch_recv, dev(rp, c, e)).wait_send()
    for q in range(QN):
        part = GFS.at[:, q * QW:(q + 1) * QW]
        remote(part, part, gf_send.at[q], gf_recv.at[q], dev(rp, c, e)).wait_send()
        part = AS.at[:, q * QW:(q + 1) * QW]
        remote(part, part, ab_send.at[q], ab_recv.at[q], dev(rm, c, e)).wait_send()
    remote(P1, P1, p1_send, p1_recv, dev(r, c, e)).wait_send()
    remote(PT, PT, pt_send, pt_recv, dev(r, c, e)).wait_send()
    remote(PU, PU, p2_send, p2_recv, dev(rm, cm, e)).wait_send()


def absorb_backward(sizes, corner, te, lh, cot, vals, par):
    nr, nc, ne = sizes
    hbm = pl.BlockSpec(memory_space=pltpu.HBM)
    vmem = pl.BlockSpec(memory_space=pltpu.VMEM)
    dma = pltpu.SemaphoreType.DMA
    square = pltpu.VMEM((CHI, CHI), BF16)
    tiles = pltpu.VMEM((CHI // LANE, CHI, LANE), F32)
    charges = pltpu.VMEM((8, CHI), jnp.int32)
    scratch = [
        square, square, pltpu.VMEM((ROWS_A, CHI * HALF), BF16), square, charges, charges,
        pltpu.VMEM((CHI, CHI), F32),
        square, square, square, square, square, square,
        pltpu.VMEM((GRP * ROWS_A, LANE), F32), tiles, tiles,
        pltpu.VMEM((NX - 1, CHI // NX, CHI), BF16), pltpu.VMEM((CHI // NX, CHI), BF16),
        pltpu.VMEM((NZ * ROWS_A, CHI // 2), BF16), pltpu.VMEM((NZ * ROWS_A, CHI // 2), BF16),
        pltpu.VMEM((NZ // 2 * ROWS_A, CHI), BF16),
        pltpu.VMEM((ROWS_A, LANE), F32), pltpu.VMEM((ROWS_A, LANE), F32), pltpu.VMEM((ROWS_A, LANE), F32),
        dma((QN,)), dma((QN,)), dma, dma, dma((NBLK,)), dma, dma,
        dma((QN,)), dma((QN,)), dma((QN,)), dma((QN,)), dma, dma, dma, dma, dma, dma, dma, dma,
    ]
    return pl.pallas_call(
        functools.partial(kernel, nr, nc, ne),
        out_shape=(
            pltpu.VMEM((ROWS_A, CHI), BF16),
            pltpu.VMEM((CHI, CHI), BF16),
            pltpu.VMEM((ROWS_A, CHI * HALF), BF16),
            pltpu.VMEM((1, ROWS_A), F32),
        ),
        in_specs=[hbm, hbm, hbm, hbm, vmem, vmem],
        out_specs=(vmem, vmem, vmem, vmem),
        scratch_shapes=scratch,
        compiler_params=pltpu.CompilerParams(
            collective_id=0, has_side_effects=True, vmem_limit_bytes=58 * 1024 * 1024
        ),
    )(corner, te, lh, cot, vals, par)


def store_kernel(gc, ge, gh, gv, gc_out, ge_out, gh_out, gv_out, sem):
    def edge(k):
        return pltpu.make_async_copy(
            ge.at[at(k * ROWS_A, ROWS_A), :], ge_out.at[:, at(k * CHI, CHI)], sem.at[0])

    loop(HALF, lambda k: edge(k).start())
    rest = [
        pltpu.make_async_copy(src, dst, sem.at[1 + n])
        for n, (src, dst) in enumerate(((gh, gh_out), (gc, gc_out), (gv, gv_out)))]
    for copy in rest:
        copy.start()
    pltpu.make_async_copy(ge, ge, sem.at[0]).wait()
    for copy in rest:
        copy.wait()


def store(gc, ge, gh, gv):
    vmem = pl.BlockSpec(memory_space=pltpu.VMEM)
    hbm = pl.BlockSpec(memory_space=pltpu.HBM)
    return pl.pallas_call(
        store_kernel,
        out_shape=(
            jax.ShapeDtypeStruct((ROWS_A, CHI), BF16),
            jax.ShapeDtypeStruct((ROWS_A, HALF * CHI), BF16),
            jax.ShapeDtypeStruct((ROWS_A, CHI * HALF), BF16),
            jax.ShapeDtypeStruct((1, ROWS_A), F32),
        ),
        in_specs=[vmem] * 4,
        out_specs=(hbm,) * 4,
        scratch_shapes=[pltpu.SemaphoreType.DMA((4,))],
        compiler_params=pltpu.CompilerParams(vmem_limit_bytes=16 * 1024 * 1024),
    )(*(pltpu.with_memory_space_constraint(t, pltpu.VMEM) for t in (gc, ge, gh, gv)))


def shards(sizes, corner, top_edge, half_system, values, cotangent, parity):
    gc, ge, gh, gv = store(*absorb_backward(
        sizes, corner[0, 0], top_edge[0, 0], half_system[0, 0], cotangent[0, 0], values[0], parity[0, 0]
    ))
    return gc[None, None], ge[None, None], gh[None, None], gv[None]


def solution(mesh):
    placed = (
        P("row", "col", None, None),
        P("row", "col", "env", None),
        P("row", "col", "env", None),
        P("row", "col", None),
        P("row", "col", None, None),
        P("row", "col", None, None),
    )
    sizes = (mesh.shape["row"], mesh.shape["col"], mesh.shape["env"])
    return jax.shard_map(
        functools.partial(shards, sizes),
        mesh=mesh,
        in_specs=placed,
        out_specs=(
            P("row", "col", "env", None),
            P("row", "col", "env", None),
            P("row", "col", "env", None),
            P("row", "col", "env"),
        ),
        check_vma=False,
    )
```

```python
import functools

import jax
import jax.numpy as jnp
from jax import lax
from jax.experimental import pallas as pl
from jax.experimental.pallas import tpu as pltpu
from jax.sharding import PartitionSpec as P

CHI = 1024
HALF = 32
BLK = 128
NBLK = CHI // BLK
LANE = 128
SUB = 4
GRP = CHI // SUB
NX, NZ = 4, 8
ROWS_A = 32
QN = 4
QW = CHI // QN
KQ = HALF // QN
MESH = pl.DeviceIdType.MESH
F32 = jnp.float32
BF16 = jnp.bfloat16


def tile_mix(tiles):
    lane = lax.broadcasted_iota(jnp.int32, tiles[0].shape, 1)
    low = lane < 64
    even = (lane // 32) % 2 == 0
    roll = lambda t, by: pltpu.roll(t, by, 1)
    x0, x1, x2, x3 = tiles
    y0 = jnp.where(low, x0, roll(x2, 64))
    y2 = jnp.where(low, roll(x0, 64), x2)
    y1 = jnp.where(low, x1, roll(x3, 64))
    y3 = jnp.where(low, roll(x1, 64), x3)
    z0 = jnp.where(even, y0, roll(y1, 32))
    z1 = jnp.where(even, roll(y0, 96), y1)
    z2 = jnp.where(even, y2, roll(y3, 32))
    z3 = jnp.where(even, roll(y2, 96), y3)
    return z0, z1, z2, z3


def dot_nn(a, b):
    return lax.dot_general(a, b, (((1,), (0,)), ((), ())), preferred_element_type=F32)


def dot_nt(a, b):
    return lax.dot_general(a, b, (((1,), (1,)), ((), ())), preferred_element_type=F32)


def dot_tn(a, b):
    return lax.dot_general(a, b, (((0,), (0,)), ((), ())), preferred_element_type=F32)


def at(start, size):
    return pl.ds(pl.multiple_of(start, size), size)


def loop(n, body):
    lax.fori_loop(0, n, lambda i, c: (body(i), c)[1], 0)


def kernel(
    nr, nc, ne,
    corner, te, lh, cot, vals, par,
    gc_out, ge_out, gh_out, gv_out,
    TE, GN, LHB, CR, CH, CHR, ACC, GFS, R, G, NCP, LHM, GFM, S, LM, F, P1, P1S, PT, PU, P2, PSA, PSS, PSR,
    te_sem, ct_sem, in_sem, cn_send, cn_recv, ch_send, ch_recv,
    gf_send, gf_recv, ab_send, ab_recv, p1_send, p1_recv, pt_send, pt_recv, p2_send, p2_recv, ps_send, ps_recv,
):
    r, c, e = lax.axis_index("row"), lax.axis_index("col"), lax.axis_index("env")
    rp, rm = lax.rem(r + 1, nr), lax.rem(r + nr - 1, nr)
    cp, cm = lax.rem(c + 1, nc), lax.rem(c + nc - 1, nc)
    x, z = e // NZ, lax.rem(e, NZ)

    def dev(row, col, env):
        return {"row": row, "col": col, "env": env}

    def remote(src, dst, send, recv, where):
        return pltpu.make_async_remote_copy(
            src_ref=src, dst_ref=dst, send_sem=send, recv_sem=recv, device_id=where, device_id_type=MESH
        )

    AS, GCB = TE, CR

    barrier = pltpu.get_barrier_semaphore()

    def greet(where):
        pl.semaphore_signal(barrier, inc=1, device_id=where, device_id_type=MESH)

    def greet_env(s):
        greet(dev(rm, c, s))

    def greet_z(s):
        greet(dev(rp, cp, x * NZ + s))

    def greet_x(s):
        greet(dev(r, c, lax.rem(x + 1 + s, NX) * NZ + z))

    def turned(m):
        return lax.rem(e // (ne // QN) + m, QN)

    def load_cot(m):
        rows = at(turned(m) * QW, QW)
        pltpu.make_async_copy(cot.at[rows, :], GN.at[rows, :], ct_sem.at[turned(m)]).start()

    def load_edge(k):
        pltpu.make_async_copy(
            te.at[:, at(k * CHI, CHI)], TE.at[at(k * ROWS_A, ROWS_A), :], te_sem.at[k // KQ]
        ).start()

    loop(ne, greet_env)
    loop(NZ, greet_z)
    loop(NX - 1, greet_x)
    greet(dev(rm, cm, e))
    greet(dev(r, c, x * NZ + lax.rem(z + 1, NZ)))
    greet(dev(r, c, x * NZ + lax.rem(z + NZ - 1, NZ)))
    loop(1, load_cot)
    loop(KQ, load_edge)

    for role in range(4):
        for g in range(NBLK):
            CH[role:role + 1, g * BLK:(g + 1) * BLK] = jnp.broadcast_to(par[role:role + 1, g:g + 1], (1, BLK))

    def weigh(m):
        rows = at(turned(m) * QW, QW)
        part = GN.at[rows, :]
        pltpu.make_async_copy(part, part, ct_sem.at[turned(m)]).wait()

        def block(g):
            rows = at(turned(m) * QW + g * BLK, BLK)
            weight = jnp.broadcast_to(lax.rsqrt(vals[0:1, rows]), (BLK, BLK)).T
            charge = CH[2:3, rows]
            for t in range(NBLK):
                lanes = slice(t * BLK, (t + 1) * BLK)
                keep = charge == CH[3:4, lanes]
                GN[rows, lanes] = jnp.where(keep, weight * GN[rows, lanes].astype(F32), 0.0).astype(BF16)

        loop(QW // BLK, block)

    odd = lax.rem(x, 2)
    first = [2 * odd, 6 - 2 * odd, 2 * odd + 1, 7 - 2 * odd]
    right, left = lax.rem(x + 1, NX), lax.rem(x + NX - 1, NX)
    near = jnp.where(odd == 0, right, left)
    far = jnp.where(odd == 0, left, right)

    def send_corner():
        for g in first:
            rows = at(g * BLK, BLK)
            remote(corner.at[rows, :], CR.at[rows, :], cn_send, cn_recv.at[g], dev(rp, cp, e)).start()

    def forward_corner():
        for n, g in enumerate(first):
            part = CR.at[at(g * BLK, BLK), :]
            to = dev(r, c, (near if n % 2 == 0 else far) * NZ + z)
            copy = remote(part, part, cn_send, cn_recv.at[g], to)
            copy.wait_recv()
            copy.start()

    def edge_rows(q, m):
        rows = at(turned(m) * QW, QW)
        cols = at(q * QW, QW)
        GFS[rows, cols] = dot_nt(GN[rows, :], TE[cols, :]).astype(BF16)

    def send_full(q, m):
        def send(j):
            s = turned(m) * (ne // QN) + lax.rem(e + j, ne // QN)
            remote(
                GFS.at[at(s * ROWS_A, ROWS_A), at(q * QW, QW)], R.at[at(e * ROWS_A, ROWS_A), at(q * QW, QW)],
                gf_send.at[q], gf_recv.at[q], dev(rp, c, s),
            ).start()

        loop(ne // QN, send)

    def edge_ready(q):
        whole = TE.at[at(q * QW, QW), :]
        pltpu.make_async_copy(whole, whole, te_sem.at[q]).wait()

    weigh(0)
    edge_ready(0)
    edge_rows(0, 0)
    pl.semaphore_wait(barrier, ne + NZ + NX + 2)
    send_full(0, 0)
    loop(QN - 1, lambda m: load_cot(m + 1))
    loop(HALF - KQ, lambda k: load_edge(k + KQ))
    lh_copy = pltpu.make_async_copy(lh, LHB, in_sem)
    lh_copy.start()
    remote(CH, CHR, ch_send, ch_recv, dev(rp, c, e)).start()
    send_corner()

    def edge_first(m):
        weigh(m + 1)
        edge_rows(0, m + 1)
        send_full(0, m + 1)

    loop(QN - 1, edge_first)

    def edge_chunk(q):
        edge_ready(q + 1)

        def part(m):
            edge_rows(q + 1, m)
            send_full(q + 1, m)

        loop(QN, part)

    loop(QN - 1, edge_chunk)

    lh_copy.wait()

    def spread(g):
        for u in range(8):
            S[at((g * 8 + u) * ROWS_A, ROWS_A), :] = LHB[:, at((g * 8 + u) * LANE, LANE)].astype(F32)

    loop(GRP // 8, spread)

    def turn(i):
        t = S[pl.ds(i, GRP, stride=ROWS_A), :].T
        for s in range(SUB):
            for h in range(GRP // LANE):
                LM[s * (GRP // LANE) + h, pl.ds(i, HALF, stride=ROWS_A), :] = t[
                    s * HALF:(s + 1) * HALF, h * LANE:(h + 1) * LANE]

    loop(ROWS_A, turn)

    def narrow(k):
        rows = at(k * ROWS_A, ROWS_A)
        for t in range(CHI // LANE):
            LHM[rows, t * LANE:(t + 1) * LANE] = LM[t, rows, :].astype(BF16)

    loop(HALF, narrow)
    forward_corner()

    def half_chunk(q):
        cols = at(q * QW, QW)
        whole = R.at[:, cols]
        remote(whole, whole, gf_send.at[q], gf_recv.at[q], dev(rp, c, e)).wait_recv()

        def regroup(d):
            for k2 in range(KQ // 4):
                lanes = at(q * QW + k2 * LANE, LANE)
                mixed = tile_mix([
                    R[at((d * 4 + d4) * ROWS_A, ROWS_A), lanes].astype(F32) for d4 in range(4)])
                for k4 in range(4):
                    GFM[at((q * KQ + k2 * 4 + k4) * ROWS_A, ROWS_A), at(d * LANE, LANE)] = mixed[k4].astype(BF16)

        loop(CHI // LANE, regroup)

        def add(s):
            rows = at(s * GRP, GRP)
            ACC[rows, :] = ACC[rows, :] + dot_tn(LHM[cols, rows], GFM[cols, :])

        loop(SUB, add)

    def clear(g):
        rows = at(g * 32, 32)
        ACC[rows, :] = jnp.zeros((32, CHI), F32)

    loop(CHI // 32, clear)
    loop(QN - 1, half_chunk)

    remote(CHR, CHR, ch_send, ch_recv, dev(rp, c, e)).wait_recv()

    def corner_rows(g):
        rows = at(g * BLK, BLK)

        @pl.when(jnp.logical_and(g // 2 != odd, g // 2 != 3 - odd))
        def _():
            part = CR.at[rows, :]
            remote(part, part, cn_send, cn_recv.at[g], dev(rp, cp, e)).wait_recv()

        charge = CHR[0:1, rows]
        for t in range(CHI // LANE):
            lanes = slice(t * LANE, (t + 1) * LANE)
            same = charge == CHR[1:2, lanes]
            F[t, rows, :] = jnp.where(same, CR[rows, lanes].astype(F32), 0.0)
            for s in range(SUB):
                NCP[at(s * GRP + g * (BLK // SUB), BLK // SUB), lanes] = F[
                    t, pl.ds(g * BLK + s, BLK // SUB, stride=SUB), :].astype(BF16)

    loop(NBLK, corner_rows)

    def absorb_chunk(q):
        cols = at(q * QW, QW)

        def columns_of(n):
            t = dot_nn(LHM[cols, :], NCP[:, at(n * 256, 256)])
            for k2 in range(KQ // 4):
                for d2 in range(2):
                    mixed = tile_mix([
                        t[(k2 * 4 + k4) * ROWS_A:(k2 * 4 + k4 + 1) * ROWS_A, d2 * LANE:(d2 + 1) * LANE]
                        for k4 in range(4)])
                    for d4 in range(4):
                        AS[at(((n * 2 + d2) * 4 + d4) * ROWS_A, ROWS_A), at(q * QW + k2 * LANE, LANE)] = (
                            mixed[d4].astype(BF16))

        loop(CHI // 256, columns_of)

    def absorb_to(q, s):
        cols = at(q * QW, QW)
        remote(
            AS.at[at(s * ROWS_A, ROWS_A), cols], G.at[at(e * ROWS_A, ROWS_A), cols],
            ab_send.at[q], ab_recv.at[q], dev(rm, c, s),
        ).start()

    def absorb_same_x(q):
        loop(NZ, lambda j: absorb_to(q, x * NZ + lax.rem(z + j, NZ)))

    def absorb_other_x(q):
        loop(ne - NZ, lambda j: absorb_to(q, lax.rem(x + 1 + j // NZ, NX) * NZ + lax.rem(z + j, NZ)))

    absorb_chunk(0)
    absorb_other_x(0)
    absorb_same_x(0)

    half_chunk(QN - 1)

    def corner_part(s):
        def block(g):
            for h in range(CHI // LANE):
                lanes = slice(h * LANE, (h + 1) * LANE)
                same = CHR[0:1, at(g * BLK, BLK)] == CHR[1:2, lanes]
                part = ACC[at(s * GRP + g * (BLK // SUB), BLK // SUB), lanes]
                F[h, pl.ds(g * BLK + s, BLK // SUB, stride=SUB), :] = jnp.where(same, part, 0.0)

        loop(NBLK, block)

    loop(SUB, corner_part)

    remote(CR, CR, cn_send, cn_recv.at[0], dev(rp, cp, e)).wait_send()

    def corner_narrow(g):
        rows = at(g * 32, 32)
        for t in range(CHI // LANE):
            GCB[rows, t * LANE:(t + 1) * LANE] = F[t, rows, :].astype(BF16)

    loop(CHI // 32, corner_narrow)
    span = CHI // NX

    def send_x(j):
        to = lax.rem(x + 1 + j, NX)
        remote(
            GCB.at[at(to * span, span), :], P1.at[j], p1_send, p1_recv, dev(r, c, to * NZ + z)
        ).start()

    loop(NX - 1, send_x)

    def absorb_more(q):
        absorb_chunk(q + 1)
        absorb_same_x(q + 1)

    loop(QN - 1, absorb_more)
    loop(QN - 1, lambda q: absorb_other_x(q + 1))

    def pair(d):
        rows = at(d * ROWS_A, ROWS_A)
        total = PSA[...]
        for t in range(CHI // LANE):
            lanes = slice(t * LANE, (t + 1) * LANE)
            total = total + R[rows, lanes].astype(F32) * AS[rows, lanes].astype(F32)
        PSA[...] = total

    PSA[...] = jnp.zeros_like(PSA)
    loop(ne, pair)
    PSS[...] = jnp.broadcast_to(jnp.sum(PSA[...], axis=1, keepdims=True), (ROWS_A, LANE))
    ps_copy = remote(PSS, PSR, ps_send, ps_recv, dev(rm, c, e))
    ps_copy.start()

    def half_rows(q):
        cols = at(q * QW, QW)

        def half_cols(n):
            t = dot_nt(GFM[cols, :], NCP[at(n * 256, 256), :])
            for h in range(2):
                LM[n * 2 + h, cols, :] = t[:, h * LANE:(h + 1) * LANE]

        loop(CHI // 256, half_cols)

    loop(QN, half_rows)

    def turn_back(i):
        t = jnp.concatenate([
            jnp.concatenate([
                LM[s * (GRP // LANE) + h, pl.ds(i, HALF, stride=ROWS_A), :] for h in range(GRP // LANE)
            ], axis=1) for s in range(SUB)], axis=0)
        S[pl.ds(i, GRP, stride=ROWS_A), :] = t.T

    loop(ROWS_A, turn_back)

    def gather(g):
        for u in range(8):
            gh_out[:, at((g * 8 + u) * LANE, LANE)] = S[at((g * 8 + u) * ROWS_A, ROWS_A), :].astype(BF16)

    loop(GRP // 8, gather)

    remote(P1, P1, p1_send, p1_recv, dev(r, c, e)).wait_recv()

    def sum_x(g):
        rows = at(g * 32, 32)
        for t in range(CHI // LANE):
            lanes = slice(t * LANE, (t + 1) * LANE)
            mine = at(x * span + g * 32, 32)
            total = F[t, mine, :]
            for j in range(NX - 1):
                total = total + P1[j, rows, lanes].astype(F32)
            F[t, mine, :] = total
            P1S[rows, lanes] = total.astype(BF16)

    loop(span // 32, sum_x)

    wide = CHI // 2
    parts = [(h, t) for h in range(2) for t in range(NZ // 2)]
    sign = [2 * lax.rem(z, 2) - 1, 1 - 2 * lax.rem(z, 2)]

    def owner(h, t):
        return lax.rem(z + sign[h] * t + NZ, NZ)

    for h, t in parts:
        remote(
            P1S.at[at(owner(h, -1 - t) * ROWS_A, ROWS_A), h * wide:(h + 1) * wide],
            PT.at[(h * 4 + t) * ROWS_A:(h * 4 + t + 1) * ROWS_A, :],
            pt_send, pt_recv, dev(r, c, x * NZ + owner(h, -1)),
        ).start()

    def edge_grad(q):
        cols = at(q * QW, QW)
        whole = G.at[:, cols]
        remote(whole, whole, ab_send.at[q], ab_recv.at[q], dev(rm, c, e)).wait_recv()
        ge_out[cols, :] = dot_tn(G[:, cols], GN[...]).astype(BF16)

    edge_grad(0)
    remote(PT, PT, pt_send, pt_recv, dev(r, c, e)).wait_recv()
    for h, t in parts:
        rows = slice((h * 4 + t) * ROWS_A, (h * 4 + t + 1) * ROWS_A)
        mine = at(x * span + owner(h, t) * ROWS_A, ROWS_A)
        for n in range(wide // LANE):
            lanes = slice(n * LANE, (n + 1) * LANE)
            PU[rows, lanes] = (F[h * (wide // LANE) + n, mine, :] + PT[rows, lanes].astype(F32)).astype(BF16)
        remote(
            PU.at[rows, :], P2.at[t * ROWS_A:(t + 1) * ROWS_A, h * wide:(h + 1) * wide],
            p2_send, p2_recv, dev(rm, cm, x * NZ + owner(h, t)),
        ).start()

    loop(QN - 1, lambda q: edge_grad(q + 1))

    remote(P2, P2, p2_send, p2_recv, dev(rm, cm, e)).wait_recv()
    for t in range(CHI // LANE):
        lanes = slice(t * LANE, (t + 1) * LANE)
        total = P2[0:ROWS_A, lanes].astype(F32)
        for j in range(1, NZ // 2):
            total = total + P2[j * ROWS_A:(j + 1) * ROWS_A, lanes].astype(F32)
        gc_out[:, lanes] = total.astype(BF16)

    ps_copy.wait_recv()
    row = lax.broadcasted_iota(jnp.int32, (ROWS_A, LANE), 0)
    lane = lax.broadcasted_iota(jnp.int32, (ROWS_A, LANE), 1)
    tile = vals[0:1, at((e // (LANE // ROWS_A)) * LANE, LANE)]
    mine = lane == row + lax.rem(e, LANE // ROWS_A) * ROWS_A
    value = jnp.sum(jnp.where(mine, jnp.broadcast_to(tile, (ROWS_A, LANE)), 0.0), axis=1, keepdims=True)
    grads = -0.5 * PSR[...] / value
    gv_out[...] = jnp.sum(jnp.where(lane == row, grads, 0.0), axis=0, keepdims=True)[:, :ROWS_A]

    ps_copy.wait_send()
    remote(CH, CHR, ch_send, ch_recv, dev(rp, c, e)).wait_send()
    for q in range(QN):
        part = GFS.at[:, q * QW:(q + 1) * QW]
        remote(part, part, gf_send.at[q], gf_recv.at[q], dev(rp, c, e)).wait_send()
        part = AS.at[:, q * QW:(q + 1) * QW]
        remote(part, part, ab_send.at[q], ab_recv.at[q], dev(rm, c, e)).wait_send()
    remote(P1, P1, p1_send, p1_recv, dev(r, c, e)).wait_send()
    remote(PT, PT, pt_send, pt_recv, dev(r, c, e)).wait_send()
    remote(PU, PU, p2_send, p2_recv, dev(rm, cm, e)).wait_send()


def absorb_backward(sizes, corner, te, lh, cot, vals, par):
    nr, nc, ne = sizes
    hbm = pl.BlockSpec(memory_space=pltpu.HBM)
    vmem = pl.BlockSpec(memory_space=pltpu.VMEM)
    dma = pltpu.SemaphoreType.DMA
    square = pltpu.VMEM((CHI, CHI), BF16)
    tiles = pltpu.VMEM((CHI // LANE, CHI, LANE), F32)
    charges = pltpu.VMEM((8, CHI), jnp.int32)
    scratch = [
        square, square, pltpu.VMEM((ROWS_A, CHI * HALF), BF16), square, charges, charges,
        pltpu.VMEM((CHI, CHI), F32),
        square, square, square, square, square, square,
        pltpu.VMEM((GRP * ROWS_A, LANE), F32), tiles, tiles,
        pltpu.VMEM((NX - 1, CHI // NX, CHI), BF16), pltpu.VMEM((CHI // NX, CHI), BF16),
        pltpu.VMEM((NZ * ROWS_A, CHI // 2), BF16), pltpu.VMEM((NZ * ROWS_A, CHI // 2), BF16),
        pltpu.VMEM((NZ // 2 * ROWS_A, CHI), BF16),
        pltpu.VMEM((ROWS_A, LANE), F32), pltpu.VMEM((ROWS_A, LANE), F32), pltpu.VMEM((ROWS_A, LANE), F32),
        dma((QN,)), dma((QN,)), dma, dma, dma((NBLK,)), dma, dma,
        dma((QN,)), dma((QN,)), dma((QN,)), dma((QN,)), dma, dma, dma, dma, dma, dma, dma, dma,
    ]
    return pl.pallas_call(
        functools.partial(kernel, nr, nc, ne),
        out_shape=(
            pltpu.VMEM((ROWS_A, CHI), BF16),
            pltpu.VMEM((CHI, CHI), BF16),
            pltpu.VMEM((ROWS_A, CHI * HALF), BF16),
            pltpu.VMEM((1, ROWS_A), F32),
        ),
        in_specs=[hbm, hbm, hbm, hbm, vmem, vmem],
        out_specs=(vmem, vmem, vmem, vmem),
        scratch_shapes=scratch,
        compiler_params=pltpu.CompilerParams(
            collective_id=0, has_side_effects=True, vmem_limit_bytes=58 * 1024 * 1024
        ),
    )(corner, te, lh, cot, vals, par)


def store_kernel(gc, ge, gh, gv, gc_out, ge_out, gh_out, gv_out, sem):
    def edge(k):
        return pltpu.make_async_copy(
            ge.at[at(k * ROWS_A, ROWS_A), :], ge_out.at[:, at(k * CHI, CHI)], sem.at[0])

    loop(HALF, lambda k: edge(k).start())
    rest = [
        pltpu.make_async_copy(src, dst, sem.at[1 + n])
        for n, (src, dst) in enumerate(((gh, gh_out), (gc, gc_out), (gv, gv_out)))]
    for copy in rest:
        copy.start()
    pltpu.make_async_copy(ge, ge, sem.at[0]).wait()
    for copy in rest:
        copy.wait()


def store(gc, ge, gh, gv):
    vmem = pl.BlockSpec(memory_space=pltpu.VMEM)
    hbm = pl.BlockSpec(memory_space=pltpu.HBM)
    return pl.pallas_call(
        store_kernel,
        out_shape=(
            jax.ShapeDtypeStruct((ROWS_A, CHI), BF16),
            jax.ShapeDtypeStruct((ROWS_A, HALF * CHI), BF16),
            jax.ShapeDtypeStruct((ROWS_A, CHI * HALF), BF16),
            jax.ShapeDtypeStruct((1, ROWS_A), F32),
        ),
        in_specs=[vmem] * 4,
        out_specs=(hbm,) * 4,
        scratch_shapes=[pltpu.SemaphoreType.DMA((4,))],
        compiler_params=pltpu.CompilerParams(vmem_limit_bytes=16 * 1024 * 1024),
    )(*(pltpu.with_memory_space_constraint(t, pltpu.VMEM) for t in (gc, ge, gh, gv)))


def shards(sizes, corner, top_edge, half_system, values, cotangent, parity):
    gc, ge, gh, gv = store(*absorb_backward(
        sizes, corner[0, 0], top_edge[0, 0], half_system[0, 0], cotangent[0, 0], values[0], parity[0, 0]
    ))
    return gc[None, None], ge[None, None], gh[None, None], gv[None]


def solution(mesh):
    placed = (
        P("row", "col", None, None),
        P("row", "col", "env", None),
        P("row", "col", "env", None),
        P("row", "col", None),
        P("row", "col", None, None),
        P("row", "col", None, None),
    )
    sizes = (mesh.shape["row"], mesh.shape["col"], mesh.shape["env"])
    return jax.shard_map(
        functools.partial(shards, sizes),
        mesh=mesh,
        in_specs=placed,
        out_specs=(
            P("row", "col", "env", None),
            P("row", "col", "env", None),
            P("row", "col", "env", None),
            P("row", "col", "env"),
        ),
        check_vma=False,
    )
```
